32 devices in a mesh: ctx: 4 (over y, x), fsdp: 8 (over z, core).
Axes of the slice: x: 2, y: 2, z: 4, core: 2. Of those that a mesh axis runs over, the one named last changes fastest.
Arguments:
- tokens: bfloat16 [8, 512, 2048], P('fsdp', 'ctx')
- attn_gain: float32 [2048], replicated, may hold values from 0.1 to 1.9
- query_gain: float32 [2048], replicated
- key_gain: float32 [2048], replicated
- w_query: bfloat16 [2048, 2048], P(('ctx', 'fsdp'))
- w_key: bfloat16 [2048, 2048], P(('ctx', 'fsdp'))
- w_value: bfloat16 [2048, 2048], P(('ctx', 'fsdp')), may hold values from -0.125 to 0.125
- output_weight: bfloat16 [2048, 2048], P(('ctx', 'fsdp')), may hold values from -2 to 2
- ffn_gain: float32 [2048], replicated, may hold values from 0.1 to 1.9
- router: bfloat16 [2048, 32], replicated
- experts: bfloat16 [2048, 32, 3072], P('ctx', 'fsdp')
- routes: int32 [8, 512, 8], P('fsdp', 'ctx'), may hold values from 0 to 31, all different within a row; in each aligned block of 128 rows (0 to 127, 128 to 255, ..., all dimensions but the last counted through in order) at most 34 rows name the same one
- cotangent: bfloat16 [8, 512, 2048], P('fsdp', 'ctx'), may hold values from -6 to 6
Outputs:
- output: bfloat16 [8, 512, 2048], P('fsdp', 'ctx')
- d_tokens: float32 [8, 512, 2048], P('fsdp', 'ctx')
- d_attn_gain: float32 [2048], replicated
- d_query_gain: float32 [2048], replicated
- d_key_gain: float32 [2048], replicated
- d_query: float32 [2048, 2048], P(('ctx', 'fsdp'))
- d_key: float32 [2048, 2048], P(('ctx', 'fsdp'))
- d_value: float32 [2048, 2048], P(('ctx', 'fsdp'))
- d_output: float32 [2048, 2048], P(('ctx', 'fsdp'))
- d_ffn_gain: float32 [2048], replicated
- d_router: float32 [2048, 32], replicated
- d_experts: float32 [2048, 32, 3072], P('ctx', 'fsdp')
The draws below stay inside these ranges and needn't reach their ends.
Inputs may be any that keep to these rules, and one draw needn't show every extreme that they name: `routes`: each row names 8 different experts; in each aligned block of 128 rows (the rows of one device) no expert is named by more than 34 rows, a bound that some block reaches.
All inputs are finite; a program needn't handle non-finite values.
Results may differ from the reference program's by a relative error of at most 0.017.
Values may be sent and summed in bfloat16 or wider, within the bound.
No kernel may reach another device: no remote copies, remote signals or barrier semaphores. Data moves between devices by JAX's collectives and lax.ppermute only.
A program may use at most 512 MiB of HBM per device.

```python
import math
import jax
import jax.numpy as jnp
import numpy as np
from jax import lax

D = 2048
H = 16
HD = 128
FF = 1024
TOPK = 8
TOK_DEV = 128
EXPERTS = 32
SEQ = 512
SEQS = 8
CAP = 34
N_CTX = 4
N_FSDP = 8


def draw_experts(key, part):
    base_key = jax.random.fold_in(key, 11)
    base = jnp.clip(jax.random.normal(base_key, (D, EXPERTS, 3 * FF), jnp.float32), -4.0, 4.0)
    column = jnp.arange(3 * FF)
    scale = jnp.where(column < 2 * FF, 1.0 / math.sqrt(D), 8.0 / math.sqrt(FF))
    return (base * scale[None, None, :]).astype(jnp.bfloat16)


def draw_router(key, part):
    own = jax.random.fold_in(key, 41)
    raw = jnp.clip(jax.random.normal(own, (D, EXPERTS), jnp.float32), -4.0, 4.0) * 0.01
    return raw.astype(jnp.bfloat16)


def draw_tokens(key, part):
    shape = (SEQS, SEQ, D)
    own = jax.random.fold_in(key, 51)
    base = jnp.clip(jax.random.normal(own, shape, jnp.float32), -6.0, 6.0)
    return base.astype(jnp.bfloat16)


def projection_draw(key, salt):
    own = jax.random.fold_in(key, salt)
    base = jnp.clip(jax.random.normal(own, (D, D), jnp.float32), -4.0, 4.0) / math.sqrt(D)
    return base.astype(jnp.bfloat16)


def draw_w_query(key, part):
    return projection_draw(key, 71)


def draw_w_key(key, part):
    return projection_draw(key, 72)


def gain_draw(key, salt):
    own = jax.random.fold_in(key, salt)
    values = 1.0 + 0.18 * jnp.clip(jax.random.normal(own, (D,), jnp.float32), -5.0, 5.0)
    return values.astype(jnp.float32)


def draw_query_gain(key, part):
    return gain_draw(key, 81)


def draw_key_gain(key, part):
    return gain_draw(key, 82)


def block_levels(stream_key, shape, split, least, high):
    def one(position, blocks):
        heights = jax.random.uniform(jax.random.fold_in(jax.random.fold_in(stream_key, 6), position), (blocks,), jnp.float32, least / len(split), high / len(split))
        return jnp.repeat(jnp.exp(heights), shape[position] // blocks).reshape((-1,) + (1,) * (len(shape) - position - 1))

    level = one(*split[0])
    for cut in split[1:]:
        level = level * one(*cut)
    return level


def routed_block(own_key, own, number, rows, number_of, top, bound, skew):
    ranking = jax.random.permutation(own_key, number_of)
    crowded, usual = portions_of(number_of, rows * top, bound, skew, True), portions_of(number_of, rows * top, bound, skew, False)
    places = jnp.arange(number_of)

    def named(lengths, offset_by):
        used = int((lengths > 0).sum())
        fixed = max(1, used // 4)
        moved = fixed + (places - fixed + offset_by * (used - fixed)) % max(1, number_of - fixed)
        return jnp.zeros((number_of,), jnp.int32).at[ranking[jnp.where(places < fixed, places, moved)]].set(jnp.asarray(lengths, jnp.int32))

    lengths = jnp.where(number % 4 == 0, named(crowded, number // 4), named(usual, number - number // 4 - 1))
    mixed = jax.random.permutation(jax.random.fold_in(own, 3), number_of)
    giver, sink = mixed[0:number_of // 2 * 2:2], mixed[1:number_of // 2 * 2:2]
    slack = jnp.minimum(lengths[giver] - 1, bound - lengths[sink]) // 2
    slack = jnp.where((giver == ranking[0]) | (sink == ranking[0]) | (lengths[sink] == 0), 0, jnp.maximum(slack, 0))
    moved = jax.random.randint(jax.random.fold_in(own, 4), (number_of // 2,), 0, 1 << 20) % (slack + 1)
    lengths = lengths.at[giver].add(-moved).at[sink].add(moved)
    members = jnp.searchsorted(jnp.cumsum(lengths), jnp.arange(rows * top), side="right").astype(jnp.int32)
    table = members.reshape(top, rows).T
    table = table[jax.random.permutation(jax.random.fold_in(own, 1), rows)]
    offset_by = jax.random.randint(jax.random.fold_in(own, 2), (rows, 1), 0, top)
    return jnp.take_along_axis(table, (jnp.arange(top)[None, :] + offset_by) % top, axis=1)


def portions_of(count, total, limit, lean, full):
    weights = [(1 << 20) // math.isqrt(standing ** lean) + 1 for standing in range(1, count + 1)]
    largest = limit if full else min(limit, max(-(-total // count), total * weights[0] // sum(weights)))
    least = 1 if total - largest >= count - 1 else 0
    given, surplus = [largest] + [least] * (count - 1), total - largest - least * (count - 1)
    while surplus > 0:
        movable = [i for i in range(1, count) if given[i] < largest] or [i for i in range(1, count) if given[i] < limit]
        pool, remaining = sum([weights[i] for i in movable]), surplus
        for i in movable:
            addition = min(limit - given[i], max(1, remaining * weights[i] // pool), surplus)
            given[i] = given[i] + addition
            surplus = surplus - addition
    return np.array(given)


def noise(key, extent, scale, bound, split=(), held_as=jnp.bfloat16):
    factor_of = block_levels(key, extent, split, -0.22, 0.18) if split else 1.0
    values = jax.random.normal(key, extent, jnp.float32) * scale * factor_of
    return jnp.minimum(jnp.maximum(values, -bound), bound).astype(held_as)


def setup_inputs(seed: int = 0) -> dict:
    streams_of = jax.random.split(jax.random.key(seed), 14)
    tokens = draw_tokens(jax.random.fold_in(streams_of[13], 71), 0)
    attn_gain = jnp.clip(1.0 + 0.18 * jax.random.normal(streams_of[1], (D,), jnp.float32), 0.1, 1.9)
    query_gain = draw_query_gain(jax.random.fold_in(streams_of[13], 71), 0)
    key_gain = draw_key_gain(jax.random.fold_in(streams_of[13], 71), 0)
    w_query = draw_w_query(jax.random.fold_in(streams_of[13], 71), 0)
    w_key = draw_w_key(jax.random.fold_in(streams_of[13], 71), 0)
    w_value = noise(streams_of[6], (D, D), D ** -0.5, 0.125, ((0, 32),))
    output_weight = noise(streams_of[7], (D, D), (max(D // 256, 1)) ** -0.5, 2.0, ((0, 32),))
    ffn_gain = jnp.clip(1.0 + 0.18 * jax.random.normal(streams_of[8], (D,), jnp.float32), 0.1, 1.9)
    router = draw_router(jax.random.fold_in(streams_of[13], 71), 0)
    experts = draw_experts(jax.random.fold_in(streams_of[13], 71), 0)
    routes_keys = jax.random.split(jax.random.fold_in(streams_of[11], 1), SEQS * SEQ // TOK_DEV)
    routes_turns = jax.random.permutation(jax.random.fold_in(streams_of[11], 3), SEQS * SEQ // TOK_DEV)
    routes = jax.vmap(lambda own, number: routed_block(jax.random.fold_in(streams_of[11], 2), own, number, TOK_DEV, EXPERTS, TOPK, CAP, 1))(routes_keys, routes_turns).reshape((SEQS, SEQ, TOPK))
    cotangent = noise(streams_of[12], (SEQS, SEQ, D), 1.0, 6.0, ((0, 8), (1, 4)))
    return dict(tokens=tokens, attn_gain=attn_gain, query_gain=query_gain, key_gain=key_gain, w_query=w_query, w_key=w_key, w_value=w_value, output_weight=output_weight, ffn_gain=ffn_gain, router=router, experts=experts, routes=routes, cotangent=cotangent)


epsilon = 1e-05
neg_large = -1e+30
highest_logit = lax.Precision.HIGHEST

@jax.custom_vjp
def low(v):
    return lax.optimization_barrier(v.astype(jnp.bfloat16)).astype(jnp.float32)

@jax.custom_vjp
def low_back(v):
    return v

def low_keep(v):
    return (low(v), None)

def low_pass(kept, grad):
    return (grad,)

def back_keep(v):
    return (v, None)

def back_low(kept, grad):
    return (low(grad),)
low.defvjp(low_keep, low_pass)
low_back.defvjp(back_keep, back_low)

def rms_norm(values, gain):
    return values * lax.rsqrt(lax.optimization_barrier(jnp.mean(values * values, -1, keepdims=True)) + epsilon) * gain

def balanced_positions(seq_length):
    index = jnp.arange(seq_length, dtype=jnp.int32)
    half_rows = TOK_DEV // 2
    device = (index // TOK_DEV).astype(jnp.int32)
    within = (index % TOK_DEV).astype(jnp.int32)
    low_pos = device * half_rows + within
    high_pos = seq_length - (device + 2) * half_rows + within
    return jnp.where(within < half_rows, low_pos, high_pos).astype(jnp.int32)

def rope_tables(positions, head_size):
    half_size = head_size // 2
    inverse_freq = jnp.exp(jnp.arange(half_size, dtype=jnp.float32) * (-2.0 * math.log(10000.0) / head_size))
    angles = positions.astype(jnp.float32)[:, None] * inverse_freq[None, :]
    cosine = jnp.cos(angles)
    sine = jnp.sin(angles)
    return (jnp.concatenate([cosine, cosine], -1), jnp.concatenate([sine, sine], -1))

def rotate(values, cosine, sine):
    half_size = values.shape[-1] // 2
    turned = jnp.concatenate([-values[..., half_size:], values[..., :half_size]], -1)
    return values * cosine[:, None, :] + turned * sine[:, None, :]

def attend_sequence(queries, keys, values, positions):
    seq_length = queries.shape[0]
    block = min(512, seq_length)
    scale = 1.0 / math.sqrt(HD)

    @jax.checkpoint
    def one_block(item):
        query_block, query_pos = item
        scores = jnp.einsum('qhd,khd->hqk', query_block, keys, precision=highest_logit) * scale
        scores = low_back(scores)
        allowed = positions[None, :] <= query_pos[:, None]
        scores = jnp.where(allowed[None], scores, neg_large)
        weights = low(jax.nn.softmax(scores, -1))
        return jnp.einsum('hqk,khd->qhd', weights, values, precision=highest_logit)
    blocks = queries.reshape(seq_length // block, block, H, HD)
    pos_blocks = positions.reshape(seq_length // block, block)
    return lax.map(one_block, (blocks, pos_blocks)).reshape(seq_length, H, HD)

def mixture(ffn_in, probs, experts, route_ids):
    token_count = ffn_in.shape[0]
    flat_ids = route_ids.reshape(-1).astype(jnp.int32)
    route_total = flat_ids.shape[0]
    order = jnp.argsort(flat_ids, stable=True).astype(jnp.int32)
    member = (flat_ids[:, None] == jnp.arange(EXPERTS, dtype=jnp.int32)[None, :]).astype(jnp.int32)
    counts = lax.optimization_barrier(jnp.sum(member, 0)).astype(jnp.int32)
    starts = (jnp.cumsum(counts) - counts).astype(jnp.int32)
    capacity = CAP * N_CTX * N_FSDP
    place = starts[:, None] + jnp.arange(capacity, dtype=jnp.int32)[None, :]
    valid = (jnp.arange(capacity, dtype=jnp.int32)[None, :] < counts[:, None]).astype(jnp.float32)
    picked = order[jnp.minimum(place, route_total - 1)]
    token_ids = (picked // TOPK).astype(jnp.int32)
    inverse = jnp.zeros((route_total,), jnp.int32).at[order].set(jnp.arange(route_total, dtype=jnp.int32))
    rank = (inverse - starts[flat_ids]).astype(jnp.int32)

    @jax.checkpoint
    def one_expert(item):
        weight_matrix, rows_of, keep_rows = item
        rows = low_back(ffn_in[rows_of]) * keep_rows[:, None]
        gate_up = low_back(jnp.dot(rows, weight_matrix[:, :2 * FF], precision=highest_logit))
        hidden = low(jax.nn.silu(gate_up[:, :FF]) * gate_up[:, FF:])
        return low(low_back(jnp.dot(hidden, weight_matrix[:, 2 * FF:].T, precision=highest_logit)))
    results = lax.map(one_expert, (jnp.moveaxis(experts, 1, 0), token_ids, valid))
    by_route = results.reshape(EXPERTS * capacity, -1)[flat_ids * capacity + rank]
    route_weight = jnp.take_along_axis(probs, route_ids, 1)
    return lax.optimization_barrier(jnp.sum(route_weight[:, :, None] * by_route.reshape(token_count, TOPK, -1), 1))

def forward(tokens, attn_gain, query_gain, key_gain, w_query, w_key, w_value, output_weight, ffn_gain, router, experts, routes):
    seq_count, seq_length, model_width = tokens.shape
    normalized_rows = low(rms_norm(tokens, attn_gain))

    def project(weight_matrix):
        return jnp.einsum('fur,rp->fup', normalized_rows, weight_matrix, precision=highest_logit)
    raw_query = low_back(project(w_query))
    raw_key = low_back(project(w_key))
    value_low = low(low_back(project(w_value)))
    positions = balanced_positions(seq_length)
    cosine, sine = rope_tables(positions, HD)
    query_rot = low(rotate(rms_norm(raw_query, query_gain).reshape(seq_count, seq_length, H, HD), cosine, sine))
    key_rot = low(rotate(rms_norm(raw_key, key_gain).reshape(seq_count, seq_length, H, HD), cosine, sine))
    value_heads = value_low.reshape(seq_count, seq_length, H, HD)

    def per_sequence(item):
        return attend_sequence(item[0], item[1], item[2], positions)
    mixed = lax.map(per_sequence, (query_rot, key_rot, value_heads))
    attended_rows = low(low_back(mixed.reshape(seq_count, seq_length, model_width)))
    hidden_after_attention = tokens + low_back(jnp.einsum('fur,rp->fup', attended_rows, output_weight, precision=highest_logit))
    ffn_in = low(rms_norm(hidden_after_attention, ffn_gain)).reshape(seq_count * seq_length, model_width)
    logits = low_back(jnp.dot(ffn_in, router, precision=highest_logit))
    probs = jax.nn.softmax(logits, -1)
    routed = mixture(ffn_in, probs, experts, routes.reshape(seq_count * seq_length, TOPK))
    return hidden_after_attention + routed.reshape(seq_count, seq_length, model_width)

def reference(tokens, attn_gain, query_gain, key_gain, w_query, w_key, w_value, output_weight, ffn_gain, router, experts, routes, cotangent):
    floats = (tokens.astype(jnp.float32), attn_gain.astype(jnp.float32), query_gain.astype(jnp.float32), key_gain.astype(jnp.float32), w_query.astype(jnp.float32), w_key.astype(jnp.float32), w_value.astype(jnp.float32), output_weight.astype(jnp.float32), ffn_gain.astype(jnp.float32), router.astype(jnp.float32), experts.astype(jnp.float32))

    def run(*arrays):
        return forward(*arrays, routes)
    result, pull = jax.vjp(run, *floats)
    grads = pull(cotangent.astype(jnp.float32))
    return (result.astype(jnp.bfloat16), grads[0], grads[1], grads[2], grads[3], grads[4], grads[5], grads[6], grads[7], grads[8], grads[9], grads[10])
```

```python
import math

import jax
import jax.numpy as jnp
from jax import lax
from jax.sharding import PartitionSpec as P

H = 16
HD = 128

epsilon = 1e-05
neg_large = -1e30
f32 = jnp.float32
bf16 = jnp.bfloat16
everyone = ("fsdp", "ctx")


def mm(a, b):
    return jnp.dot(a, b, preferred_element_type=f32)


def mm_nt(a, b):
    return lax.dot_general(a, b, (((1,), (1,)), ((), ())), preferred_element_type=f32)


def mm_tn(a, b):
    return lax.dot_general(a, b, (((0,), (0,)), ((), ())), preferred_element_type=f32)


def exact_mm(a, b):
    return jnp.dot(a, b, precision=lax.Precision.HIGHEST, preferred_element_type=f32)


def inv_rms(values):
    return lax.rsqrt(jnp.mean(values * values, -1, keepdims=True) + epsilon)


def norm_back(grad, values, scale, gain):
    weighted = grad * gain
    grad_values = scale * weighted - values * scale * scale * scale * jnp.mean(
        weighted * values, -1, keepdims=True
    )
    grad_gain = jnp.sum(grad * values * scale, axis=0)
    return (grad_values, grad_gain)


def rope_tables(positions, head_size):
    half_size = head_size // 2
    inverse_freq = jnp.exp(
        jnp.arange(half_size, dtype=f32) * (-2.0 * math.log(10000.0) / head_size)
    )
    angles = positions.astype(f32)[:, None] * inverse_freq[None, :]
    cosine = jnp.cos(angles)
    sine = jnp.sin(angles)
    return (jnp.concatenate([cosine, cosine], -1), jnp.concatenate([sine, sine], -1))


def rotate(values, cosine, sine):
    half_size = values.shape[-1] // 2
    turned = jnp.concatenate([-values[..., half_size:], values[..., :half_size]], -1)
    return values * cosine[:, None, :] + turned * sine[:, None, :]


def rotate_back(grad, cosine, sine):
    half_size = grad.shape[-1] // 2
    turned = jnp.concatenate([grad[..., half_size:], -grad[..., :half_size]], -1)
    return grad * cosine[:, None, :] + turned * sine[:, None, :]


def from_peer(values, offset, total):
    return lax.ppermute(values, "ctx", [(i, i ^ offset) for i in range(total)])


def gather_rows(values, total):
    return jnp.concatenate(
        [values] + [from_peer(values, j, total) for j in range(1, total)], 0
    )


def scatter_rows(partial, total):
    rows = partial.shape[0] // total
    result = partial[:rows]
    for j in range(1, total):
        piece = partial[j * rows : (j + 1) * rows].astype(bf16)
        result = result + from_peer(piece, j, total).astype(f32)
    return result


def sum_rows(values, total):
    count, width = values.shape
    rows = width // total
    result = values
    for j in range(1, total):
        other = from_peer(values, j, total).reshape(count, total, rows)
        other = jnp.stack([other[:, i ^ j] for i in range(total)], 1)
        result = result + other.reshape(count, width)
    return result


def body(
    tokens,
    attn_gain,
    query_gain,
    key_gain,
    w_query,
    w_key,
    w_value,
    output_weight,
    ffn_gain,
    router,
    experts,
    routes,
    cotangent,
):
    row_total = tokens.shape[1]
    half_rows = row_total // 2
    model_width = tokens.shape[2]
    expert_total = router.shape[1]
    slice_rows = experts.shape[0]
    local_experts = experts.shape[1]
    top_count = routes.shape[2]
    ff = experts.shape[2] // 3
    C = lax.axis_size("ctx")
    F = lax.axis_size("fsdp")
    devices = C * F
    W = model_width // C
    heads = H // C
    seq = C * row_total
    shard = w_query.shape[0]
    pieces = C // local_experts
    cap_unit = 16 * expert_total * pieces
    piece_cap = (17 * row_total * top_count + cap_unit - 1) // cap_unit
    capacity = pieces * piece_cap
    slots = expert_total * capacity
    me = lax.axis_index("ctx")
    row = lax.axis_index("fsdp")
    my_expert = row * local_experts + me // pieces
    my_column = me * W

    tokens_low = tokens.reshape(row_total, model_width)
    tokens_seq = gather_rows(tokens_low, C)

    def by_column(weight):
        return jnp.swapaxes(weight.reshape(shard, C, W), 0, 1)

    w_cols = lax.all_to_all(
        jnp.concatenate([by_column(w_query), by_column(w_key), by_column(w_value)], 2),
        "ctx",
        split_axis=0,
        concat_axis=0,
        tiled=True,
    )
    w_qk = lax.all_gather(w_cols[:, :, : 2 * W], "fsdp", axis=1, tiled=True).reshape(
        model_width, 2 * W
    )
    w_v = lax.all_gather(w_cols[:, :, 2 * W :], "fsdp", axis=1, tiled=True).reshape(model_width, W)
    w_o = lax.all_gather(output_weight, "fsdp", axis=0, tiled=True)

    own = []
    for j in range(C):
        piece = lax.dynamic_index_in_dim(experts, (me ^ j) // pieces, 1, keepdims=False)
        own.append(piece if j == 0 else from_peer(piece, j, C))
    expert = jnp.zeros((C, slice_rows, 3 * ff), bf16)
    for j in range(C):
        expert = lax.dynamic_update_slice_in_dim(expert, own[j][None], me ^ j, 0)
    expert = expert.reshape(model_width, 3 * ff)

    route_ids = routes.reshape(row_total, top_count)
    member = jnp.sum(
        (route_ids[:, :, None] == jnp.arange(expert_total, dtype=jnp.int32)).astype(f32), 1
    )
    order = jnp.arange(row_total, dtype=jnp.int32)
    earlier = mm((order[None, :] < order[:, None]).astype(bf16), member.astype(bf16))
    marked = jnp.where(member > 0.5, earlier, -1.0)
    slot_ids = jnp.arange(slots, dtype=jnp.int32)
    slot_expert = (
        slot_ids[:, None] // capacity == jnp.arange(expert_total, dtype=jnp.int32)[None, :]
    ).astype(bf16)
    slot_rank = mm_nt(slot_expert, marked.astype(bf16))
    chosen = slot_rank == (slot_ids % capacity).astype(f32)[:, None]
    select = chosen.astype(bf16)

    def send_rows(values):
        moved = lax.all_to_all(
            values.reshape(devices, piece_cap, model_width // 128, 128),
            everyone,
            split_axis=0,
            concat_axis=0,
            tiled=True,
        )
        return moved.reshape(slots, model_width)

    cot_low = cotangent.reshape(row_total, model_width)
    cot_rows = send_rows(mm(select, cot_low).astype(bf16))

    place = me ^ jnp.arange(C, dtype=jnp.int32)
    within = jnp.arange(half_rows, dtype=jnp.int32)
    positions = jnp.concatenate(
        [
            place[:, None] * half_rows + within,
            (2 * C - 1 - place)[:, None] * half_rows + within,
        ],
        1,
    ).reshape(seq)
    cosine, sine = rope_tables(positions, HD)
    inputs_seq = tokens_seq.astype(f32)
    scale_one = inv_rms(inputs_seq)
    normed = (inputs_seq * scale_one * attn_gain).astype(bf16)
    gain_q = lax.dynamic_slice_in_dim(query_gain, my_column, W)
    gain_k = lax.dynamic_slice_in_dim(key_gain, my_column, W)
    raw_qk = mm(normed, w_qk)
    value_low = mm(normed, w_v).astype(bf16)
    raw_q = raw_qk[:, :W]
    raw_k = raw_qk[:, W:]
    squares = sum_rows(jnp.stack([jnp.sum(raw_q * raw_q, -1), jnp.sum(raw_k * raw_k, -1)]), C)
    scales = lax.rsqrt(squares / model_width + epsilon)
    scale_q = scales[0][:, None]
    scale_k = scales[1][:, None]
    query_rot = rotate((raw_q * scale_q * gain_q).reshape(seq, heads, HD), cosine, sine).astype(
        bf16
    )
    key_rot = rotate((raw_k * scale_k * gain_k).reshape(seq, heads, HD), cosine, sine).astype(bf16)
    value_heads = value_low.reshape(seq, heads, HD)
    soft = 1.0 / math.sqrt(HD)
    scores = jnp.einsum("qhd,khd->hqk", query_rot, key_rot, preferred_element_type=f32) * soft
    allowed = positions[None, :] <= positions[:, None]
    scores = jnp.where(allowed[None], scores, neg_large)
    weights = jnp.exp(scores - jnp.max(scores, -1, keepdims=True))
    attn_probs = weights / jnp.sum(weights, -1, keepdims=True)
    prob_low = attn_probs.astype(bf16)
    attended = (
        jnp.einsum("hqk,khd->qhd", prob_low, value_heads, preferred_element_type=f32)
        .reshape(seq, W)
        .astype(bf16)
    )
    inputs = tokens_low.astype(f32)
    hidden_one = inputs + scatter_rows(mm(attended, w_o), C)

    scale_two = inv_rms(hidden_one)
    ffn_in = (hidden_one * scale_two * ffn_gain).astype(bf16)
    probs = jax.nn.softmax(mm(ffn_in, router), -1)
    rows = send_rows(mm(select, ffn_in).astype(bf16))

    w_gu = expert[:, : 2 * ff]
    w_d = expert[:, 2 * ff :]
    row_probs = jax.nn.softmax(mm(rows, router), -1)
    is_mine = jnp.arange(expert_total, dtype=jnp.int32)[None, :] == my_expert
    row_weight = jnp.sum(jnp.where(is_mine, row_probs, 0.0), -1, keepdims=True)
    gate_up = mm(rows, w_gu)
    gate = gate_up[:, :ff]
    up = gate_up[:, ff:]
    sigma = jax.nn.sigmoid(gate)
    swish = gate * sigma
    hidden_low = (swish * up).astype(bf16)
    expert_rows = mm_nt(hidden_low, w_d).astype(bf16)
    cot_f = cot_rows.astype(f32)
    row_grad_weight = jnp.sum(cot_f * expert_rows.astype(f32), -1)
    grad_rows = (row_weight * cot_f).astype(bf16)
    grad_hidden = mm(grad_rows, w_d)
    grad_gate = grad_hidden * up * sigma * (1.0 + gate * (1.0 - sigma))
    grad_gate_up = jnp.concatenate([grad_gate, grad_hidden * swish], -1).astype(bf16)
    route_back = mm_nt(grad_gate_up, w_gu).astype(bf16)
    back_weight = lax.all_to_all(
        row_grad_weight.reshape(devices, 1, piece_cap), everyone, 0, 0, tiled=True
    ).reshape(slots)
    back_rows = send_rows(route_back)
    back_out = send_rows(expert_rows)

    d_expert = jnp.concatenate([mm_tn(rows, grad_gate_up), mm_tn(grad_rows, hidden_low)], 1)
    d_parts = lax.all_to_all(
        d_expert.astype(bf16).reshape(C, slice_rows, 3 * ff), "ctx", 0, 0, tiled=True
    ).reshape(local_experts, pieces, slice_rows, 3 * ff)
    d_experts = jnp.swapaxes(jnp.sum(d_parts.astype(f32), 1), 0, 1)

    spread = exact_mm(probs, slot_expert.astype(f32).T)
    mix = jnp.where(chosen.T, spread, 0.0)
    mix_high = mix.astype(bf16)
    mix_low = (mix - mix_high.astype(f32)).astype(bf16)
    mixed = mm(mix_high, back_out) + mm(mix_low, back_out)
    output = (hidden_one + mixed).astype(bf16).reshape(1, row_total, model_width)

    grad_probs = exact_mm(jnp.where(chosen.T, back_weight[None, :], 0.0), slot_expert.astype(f32))
    grad_logits = (probs * (grad_probs - jnp.sum(probs * grad_probs, -1, keepdims=True))).astype(
        bf16
    )
    grad_ffn = mm_tn(select, back_rows) + mm_nt(grad_logits, router)
    grad_router = mm_tn(ffn_in, grad_logits)
    grad_hidden_one, grad_ffn_gain = norm_back(grad_ffn, hidden_one, scale_two, ffn_gain)
    grad_hidden_one = grad_hidden_one + cot_low.astype(f32)
    router_slice = jnp.sum(
        lax.all_to_all(
            grad_router.reshape(devices, model_width // devices, expert_total),
            everyone,
            0,
            0,
            tiled=True,
        ),
        0,
    )

    branch_seq = gather_rows(grad_hidden_one.astype(bf16), C)
    grad_att = mm_nt(branch_seq, w_o).astype(bf16).reshape(seq, heads, HD)
    d_output = lax.psum_scatter(
        mm_tn(attended, branch_seq).astype(bf16), "fsdp", scatter_dimension=0, tiled=True
    ).astype(f32)
    grad_prob = jnp.einsum("qhd,khd->hqk", grad_att, value_heads, preferred_element_type=f32)
    delta = jnp.sum(attn_probs * grad_prob, -1, keepdims=True)
    grad_scores = (attn_probs * (grad_prob - delta)).astype(bf16)
    grad_value = (
        jnp.einsum("hqk,qhd->khd", prob_low, grad_att, preferred_element_type=f32)
        .astype(bf16)
        .reshape(seq, W)
    )
    grad_q_rot = (
        jnp.einsum("hqk,khd->qhd", grad_scores, key_rot, preferred_element_type=f32) * soft
    )
    grad_k_rot = (
        jnp.einsum("hqk,qhd->khd", grad_scores, query_rot, preferred_element_type=f32) * soft
    )
    grad_q_n = rotate_back(grad_q_rot, cosine, sine).reshape(seq, W)
    grad_k_n = rotate_back(grad_k_rot, cosine, sine).reshape(seq, W)
    weighted_q = grad_q_n * gain_q
    weighted_k = grad_k_n * gain_k
    dots = (
        sum_rows(jnp.stack([jnp.sum(weighted_q * raw_q, -1), jnp.sum(weighted_k * raw_k, -1)]), C)
        / model_width
    )
    grad_q_gain = jnp.sum(grad_q_n * raw_q * scale_q, 0)
    grad_k_gain = jnp.sum(grad_k_n * raw_k * scale_k, 0)
    grad_q = (scale_q * weighted_q - raw_q * scale_q * scale_q * scale_q * dots[0][:, None]).astype(
        bf16
    )
    grad_k = (scale_k * weighted_k - raw_k * scale_k * scale_k * scale_k * dots[1][:, None]).astype(
        bf16
    )
    grad_qk = jnp.concatenate([grad_q, grad_k], 1)

    def reduce_weight(partial, width):
        return lax.psum_scatter(
            partial.astype(bf16).reshape(C, F * shard, width),
            "fsdp",
            scatter_dimension=1,
            tiled=True,
        )

    d_v_cols = reduce_weight(mm_tn(normed, grad_value), W)
    d_qk_cols = reduce_weight(mm_tn(normed, grad_qk), 2 * W)
    d_cols = lax.all_to_all(
        jnp.concatenate([d_qk_cols, d_v_cols], 2), "ctx", 0, 0, tiled=True
    ).reshape(C, shard, 3, W)
    d_qkv = jnp.transpose(d_cols, (2, 1, 0, 3)).reshape(3, shard, model_width).astype(f32)

    grad_normed = scatter_rows(mm_nt(grad_qk, w_qk) + mm_nt(grad_value, w_v), C)
    grad_inputs, grad_attn_gain = norm_back(grad_normed, inputs, scale_one[:row_total], attn_gain)
    grad_inputs = grad_inputs + grad_hidden_one

    vector = jnp.concatenate(
        [
            grad_attn_gain,
            grad_ffn_gain,
            grad_q_gain,
            grad_k_gain,
            router_slice.reshape(model_width // devices * expert_total),
        ]
    ).reshape(1, -1, 128)
    everything = lax.all_to_all(
        jnp.broadcast_to(vector, (devices,) + vector.shape[1:]), everyone, 0, 0, tiled=True
    ).reshape(devices, -1)
    d_attn_gain = jnp.sum(everything[:, :model_width], 0)
    d_ffn_gain = jnp.sum(everything[:, model_width : 2 * model_width], 0)
    by_place = jnp.sum(
        everything[:, 2 * model_width : 2 * model_width + 2 * W].reshape(F, C, 2, W), 0
    )
    d_query_gain = by_place[:, 0].reshape(model_width)
    d_key_gain = by_place[:, 1].reshape(model_width)
    d_router = everything[:, 2 * model_width + 2 * W :].reshape(model_width, expert_total)

    return (
        output,
        grad_inputs.reshape(1, row_total, model_width),
        d_attn_gain,
        d_query_gain,
        d_key_gain,
        d_qkv[0],
        d_qkv[1],
        d_qkv[2],
        d_output,
        d_ffn_gain,
        d_router,
        d_experts,
    )


def solution(mesh):
    placed = (
        P("fsdp", "ctx", None),
        P(),
        P(),
        P(),
        P(("ctx", "fsdp"), None),
        P(("ctx", "fsdp"), None),
        P(("ctx", "fsdp"), None),
        P(("ctx", "fsdp"), None),
        P(),
        P(),
        P("ctx", "fsdp", None),
        P("fsdp", "ctx", None),
        P("fsdp", "ctx", None),
    )
    return jax.shard_map(
        body,
        mesh=mesh,
        in_specs=placed,
        out_specs=(
            P("fsdp", "ctx", None),
            P("fsdp", "ctx", None),
            P(),
            P(),
            P(),
            P(("ctx", "fsdp"), None),
            P(("ctx", "fsdp"), None),
            P(("ctx", "fsdp"), None),
            P(("ctx", "fsdp"), None),
            P(),
            P(),
            P("ctx", "fsdp", None),
        ),
        check_vma=False,
    )
```

```python
import functools
import math

import jax
import jax.numpy as jnp
from jax import lax
from jax.experimental import pallas as pl
from jax.experimental.pallas import tpu as pltpu
from jax.sharding import PartitionSpec as P

HD = 128

epsilon = 1e-05
neg_large = -1e30
f32 = jnp.float32
bf16 = jnp.bfloat16
everyone = ("fsdp", "ctx")


def mm(a, b):
    return jnp.dot(a, b, preferred_element_type=f32)


def mm_nt(a, b):
    return lax.dot_general(a, b, (((1,), (1,)), ((), ())), preferred_element_type=f32)


def mm_tn(a, b):
    return lax.dot_general(a, b, (((0,), (0,)), ((), ())), preferred_element_type=f32)


def inv_rms(values):
    return lax.rsqrt(jnp.mean(values * values, -1, keepdims=True) + epsilon)


def norm_back(grad, values, scale, gain):
    weighted = grad * gain
    grad_values = scale * weighted - values * scale * scale * scale * jnp.mean(
        weighted * values, -1, keepdims=True
    )
    grad_gain = jnp.sum(grad * values * scale, axis=0)
    return (grad_values, grad_gain)


def rope_tables(positions, head_size):
    half_size = head_size // 2
    inverse_freq = jnp.exp(
        jnp.arange(half_size, dtype=f32) * (-2.0 * math.log(10000.0) / head_size)
    )
    angles = positions.astype(f32)[:, None] * inverse_freq[None, :]
    cosine = jnp.cos(angles)
    sine = jnp.sin(angles)
    return (jnp.concatenate([cosine, cosine], -1), jnp.concatenate([sine, sine], -1))


def from_peer(values, offset, total):
    return lax.ppermute(values, "ctx", [(i, i ^ offset) for i in range(total)])


def place_kernel(order, rows, block, place_ref, *refs):
    parts, whole, sems = refs[:-2], refs[-2], refs[-1]
    step = pl.program_id(0)
    copies = []
    for n, (j, half) in enumerate(order):
        first = ((place_ref[0] ^ j) * 2 + half) * rows + step * block
        first = pl.multiple_of(first, block)
        copies.append(
            pltpu.make_async_copy(parts[n], whole.at[pl.ds(first, block), :], sems.at[n])
        )
        copies[-1].start()
    for copy in copies:
        copy.wait()


def place_parts(place, order, parts):
    rows, width = parts[0].shape
    block = min(64, rows)
    steps = rows // block
    return pl.pallas_call(
        functools.partial(place_kernel, order, rows, block),
        grid_spec=pltpu.PrefetchScalarGridSpec(
            num_scalar_prefetch=1,
            grid=(steps,),
            in_specs=[pl.BlockSpec((block, width), lambda i, s: (i, 0))] * len(parts),
            out_specs=pl.BlockSpec(memory_space=pl.ANY),
            scratch_shapes=[pltpu.SemaphoreType.DMA((len(parts),))],
        ),
        out_shape=jax.ShapeDtypeStruct((len(parts) * rows, width), parts[0].dtype),
        compiler_params=pltpu.CompilerParams(vmem_limit_bytes=30 << 20),
        cost_estimate=pl.CostEstimate(
            flops=0, bytes_accessed=4 * len(parts) * rows * width, transcendentals=0
        ),
        name="place_parts",
    )(place, *parts)


def merge_kernel(steps, block, total, pieces, base, place_ref, *refs):
    parts, whole, held, sems = refs[: total * pieces], refs[-3], refs[-2], refs[-1]
    step = pl.program_id(0)
    slot = lax.rem(step, 2)

    def copy(at, side, m):
        rows = pl.ds(pl.multiple_of(base + at * block, block), block)
        return pltpu.make_async_copy(
            held.at[side, m], whole.at[rows, place_ref[0] ^ m, :], sems.at[side, m]
        )

    for m in range(total):

        @pl.when(step >= 2)
        def _():
            copy(step - 2, slot, m).wait()

        value = parts[m * pieces][...].astype(f32)
        for p in range(1, pieces):
            value = value + parts[m * pieces + p][...].astype(f32)
        held[slot, m] = value
        copy(step, slot, m).start()

    @pl.when(step == steps - 1)
    def _():
        for m in range(total):
            if steps >= 2:
                copy(step - 1, 1 - slot, m).wait()
            copy(step, slot, m).wait()


def merge_parts(place, parts, total, base, rows_total, whole=None):
    rows, width = parts[0].shape
    pieces = len(parts) // total
    block = min(64, rows)
    steps = rows // block
    more = [] if whole is None else [whole]
    return pl.pallas_call(
        functools.partial(merge_kernel, steps, block, total, pieces, base),
        grid_spec=pltpu.PrefetchScalarGridSpec(
            num_scalar_prefetch=1,
            grid=(steps,),
            in_specs=[pl.BlockSpec((block, width), lambda i, s: (i, 0))] * len(parts)
            + [pl.BlockSpec(memory_space=pl.ANY)] * len(more),
            out_specs=pl.BlockSpec(memory_space=pl.ANY),
            scratch_shapes=[
                pltpu.VMEM((2, total, block, width), f32),
                pltpu.SemaphoreType.DMA((2, total)),
            ],
        ),
        out_shape=jax.ShapeDtypeStruct((rows_total, total, width), f32),
        input_output_aliases={1 + len(parts): 0} if more else {},
        compiler_params=pltpu.CompilerParams(vmem_limit_bytes=30 << 20),
        cost_estimate=pl.CostEstimate(
            flops=0,
            bytes_accessed=2 * len(parts) * rows * width + 4 * total * rows * width,
            transcendentals=0,
        ),
        name="merge_parts",
    )(place, *parts, *more)


def gather_rows(values, total):
    return jnp.concatenate(
        [values] + [from_peer(values, j, total) for j in range(1, total)], 0
    )


def scatter_rows(partial, total):
    rows = partial.shape[0] // total
    result = partial[:rows]
    for j in range(1, total):
        piece = partial[j * rows : (j + 1) * rows].astype(bf16)
        result = result + from_peer(piece, j, total).astype(f32)
    return result


def sum_rows(values, total):
    count, width = values.shape
    bits = total.bit_length() - 1
    result = values
    for j in range(1, total):
        other = from_peer(values, j, total).reshape((count,) + (2,) * bits + (width // total,))
        other = jnp.flip(other, [1 + n for n in range(bits) if j >> (bits - 1 - n) & 1])
        result = result + other.reshape(count, width)
    return result


def dot_nn(a, b):
    return lax.dot_general(a, b, (((1,), (0,)), ((), ())), preferred_element_type=f32)


def expert_kernel(
    steps,
    mine_ref,
    rows_ref,
    cots_ref,
    router_ref,
    gate_w,
    up_w,
    down_w,
    back_ref,
    out_ref,
    grads_ref,
    ggate_ref,
    gup_ref,
    hidden_ref,
    total_out,
    total_back,
    weight,
):
    step = pl.program_id(0)
    mine = mine_ref[0]
    width = rows_ref.shape[1]
    expert_total = router_ref.shape[1]

    @pl.when(step == 0)
    def _():
        logits = dot_nn(rows_ref[...], router_ref[...])
        logits = jnp.exp(logits - jnp.max(logits, -1, keepdims=True))
        column = lax.broadcasted_iota(jnp.int32, logits.shape, 1)
        chosen = jnp.sum(jnp.where(column == mine, logits, 0.0), -1, keepdims=True)
        weight[...] = chosen / jnp.sum(logits, -1, keepdims=True)
        grads_ref[...] = (weight[...] * cots_ref[...].astype(f32)).astype(bf16)
        total_out[...] = jnp.zeros_like(total_out)
        total_back[...] = jnp.zeros_like(total_back)

    gate = dot_nn(rows_ref[...], gate_w[...])
    up = dot_nn(rows_ref[...], up_w[...])
    grad_hidden = dot_nn(grads_ref[...], down_w[...])
    sigma = jax.nn.sigmoid(gate)
    swish = gate * sigma
    hidden = (swish * up).astype(bf16)
    grad_gate = (grad_hidden * up * sigma * (1.0 + gate * (1.0 - sigma))).astype(bf16)
    grad_up = (grad_hidden * swish).astype(bf16)
    hidden_ref[...] = hidden
    ggate_ref[...] = grad_gate
    gup_ref[...] = grad_up
    total_out[...] += mm_nt(hidden, down_w[...])
    total_back[...] += mm_nt(grad_gate, gate_w[...]) + mm_nt(grad_up, up_w[...])

    @pl.when(step == steps - 1)
    def _():
        result = total_out[...].astype(bf16).astype(f32)
        out_ref[...] = (weight[...] * result).astype(bf16)
        grad_weight = jnp.sum(cots_ref[...].astype(f32) * result, -1, keepdims=True)
        high = grad_weight.astype(bf16).astype(f32)
        low = grad_weight - high
        back_ref[:, :width] = total_back[...].astype(bf16)
        extra = back_ref.shape[1] - width
        column = lax.broadcasted_iota(jnp.int32, (rows_ref.shape[0], extra), 1)
        side = jnp.where(column == mine, high, 0.0) + jnp.where(
            column == expert_total + mine, low, 0.0
        )
        back_ref[:, width:] = side.astype(bf16)


def run_expert(mine, rows, cots, router, expert, extra):
    count, width = rows.shape
    ff = expert.shape[1] // 3
    block = min(256, ff)
    steps = ff // block
    whole = pl.BlockSpec((count, width), lambda i, s: (0, 0))
    part = pl.BlockSpec((count, block), lambda i, s: (0, i))
    return pl.pallas_call(
        functools.partial(expert_kernel, steps),
        grid_spec=pltpu.PrefetchScalarGridSpec(
            num_scalar_prefetch=1,
            grid=(steps,),
            in_specs=[
                whole,
                whole,
                pl.BlockSpec(router.shape, lambda i, s: (0, 0)),
                pl.BlockSpec((width, block), lambda i, s: (0, i)),
                pl.BlockSpec((width, block), lambda i, s: (0, steps + i)),
                pl.BlockSpec((width, block), lambda i, s: (0, 2 * steps + i)),
            ],
            out_specs=[
                pl.BlockSpec((count, width + extra), lambda i, s: (0, 0)),
                whole,
                whole,
                part,
                part,
                part,
            ],
            scratch_shapes=[
                pltpu.VMEM((count, width), f32),
                pltpu.VMEM((count, width), f32),
                pltpu.VMEM((count, 1), f32),
            ],
        ),
        out_shape=[
            jax.ShapeDtypeStruct((count, width + extra), bf16),
            jax.ShapeDtypeStruct((count, width), bf16),
            jax.ShapeDtypeStruct((count, width), bf16),
            jax.ShapeDtypeStruct((count, ff), bf16),
            jax.ShapeDtypeStruct((count, ff), bf16),
            jax.ShapeDtypeStruct((count, ff), bf16),
        ],
        compiler_params=pltpu.CompilerParams(vmem_limit_bytes=48 << 20),
        cost_estimate=pl.CostEstimate(
            flops=12 * count * width * ff,
            bytes_accessed=6 * width * ff + 10 * count * width,
            transcendentals=count * ff,
        ),
        name="expert",
    )(mine, rows, cots, router, expert, expert, expert)


def weight_kernel(groups, steps, place_ref, *refs):
    step = pl.program_id(0)

    def total(left, right):
        result = mm_tn(refs[left][...], refs[right][...])
        for g in range(1, groups):
            result = result + mm_tn(refs[5 * g + left][...], refs[5 * g + right][...])
        half = refs[-1].shape[0]
        refs[-2][...] = result[:half].astype(bf16)
        refs[-1][...] = result[half:].astype(bf16)

    @pl.when(step < steps)
    def _():
        total(0, 2)

    @pl.when((step >= steps) & (step < 2 * steps))
    def _():
        total(0, 3)

    @pl.when(step >= 2 * steps)
    def _():
        total(1, 4)


def weight_grad(place, groups, columns):
    count, _ = groups[0][0].shape
    ff = groups[0][2].shape[1]
    block = min(512, ff)
    steps = ff // block
    side = pl.BlockSpec((count, columns), lambda i, s: (0, s[0]))

    def part(first):
        return pl.BlockSpec(
            (count, block),
            lambda i, s: (0, jnp.clip(i - first * steps, 0, steps - 1)),
        )

    return pl.pallas_call(
        functools.partial(weight_kernel, len(groups), steps),
        grid_spec=pltpu.PrefetchScalarGridSpec(
            num_scalar_prefetch=1,
            grid=(3 * steps,),
            in_specs=[side, side, part(0), part(1), part(2)] * len(groups),
            out_specs=[pl.BlockSpec((columns // 2, block), lambda i, s: (0, i))] * 2,
        ),
        out_shape=[jax.ShapeDtypeStruct((columns // 2, 3 * ff), bf16)] * 2,
        compiler_params=pltpu.CompilerParams(vmem_limit_bytes=48 << 20),
        cost_estimate=pl.CostEstimate(
            flops=6 * len(groups) * count * columns * ff,
            bytes_accessed=6 * columns * ff + 10 * len(groups) * count * ff,
            transcendentals=0,
        ),
        name="weight_grad",
    )(place, *[a for group in groups for a in group])


def collect_kernel(total, *refs):
    result = dot_nn(refs[0][...], refs[total][...])
    for j in range(1, total):
        result = result + dot_nn(refs[j][...], refs[total + j][...])
    refs[-1][...] = result.astype(bf16)


def collect_rows(places, parts):
    tokens = places[0].shape[0]
    rows, width = parts[0].shape
    block = 512 if width % 512 == 0 else 768
    return pl.pallas_call(
        functools.partial(collect_kernel, len(parts)),
        grid=(pl.cdiv(width, block),),
        in_specs=[pl.BlockSpec((tokens, rows), lambda i: (0, 0))] * len(parts)
        + [pl.BlockSpec((rows, block), lambda i: (0, i))] * len(parts),
        out_specs=pl.BlockSpec((tokens, block), lambda i: (0, i)),
        out_shape=jax.ShapeDtypeStruct((tokens, width), bf16),
        compiler_params=pltpu.CompilerParams(vmem_limit_bytes=48 << 20),
        cost_estimate=pl.CostEstimate(
            flops=2 * len(parts) * tokens * rows * width,
            bytes_accessed=2 * len(parts) * rows * (width + tokens) + 2 * tokens * width,
            transcendentals=0,
        ),
        name="collect_rows",
    )(*places, *parts)


def turn(values, cosine, sine):
    return values * cosine + pltpu.roll(values, HD // 2, 1) * sine


def head_forward(raw_q, raw_k, scale, gains, cosine, sine, row_pos, col_pos):
    query = turn(raw_q * scale[:, 0:1] * gains[0:1, :], cosine, sine).astype(bf16)
    key = turn(raw_k * scale[:, 1:2] * gains[1:2, :], cosine, sine).astype(bf16)
    scores = mm_nt(query, key) * (1.0 / math.sqrt(HD))
    scores = jnp.where(col_pos <= row_pos, scores, neg_large)
    weights = jnp.exp(scores - jnp.max(scores, -1, keepdims=True))
    return query, key, weights / jnp.sum(weights, -1, keepdims=True)


def attend_kernel(q_ref, k_ref, v_ref, scale_ref, gain_ref, cos_ref, sin_ref, rp, cp, out_ref):
    _, _, probs = head_forward(
        q_ref[...],
        k_ref[...],
        scale_ref[...],
        gain_ref[...],
        cos_ref[...],
        sin_ref[...],
        rp[...],
        cp[...],
    )
    out_ref[...] = dot_nn(probs.astype(bf16), v_ref[...].astype(bf16)).astype(bf16)


def attend_back_kernel(
    q_ref,
    k_ref,
    v_ref,
    scale_ref,
    gain_ref,
    cos_ref,
    sin_ref,
    rp,
    cp,
    grad_ref,
    yq_ref,
    yk_ref,
    gv_ref,
    dots_ref,
    gains_ref,
):
    raw_q = q_ref[...]
    raw_k = k_ref[...]
    scale = scale_ref[...]
    gains = gain_ref[...]
    query, key, probs = head_forward(
        raw_q, raw_k, scale, gains, cos_ref[...], sin_ref[...], rp[...], cp[...]
    )
    grad = grad_ref[...]
    grad_prob = mm_nt(grad, v_ref[...].astype(bf16))
    delta = jnp.sum(probs * grad_prob, -1, keepdims=True)
    grad_scores = (probs * (grad_prob - delta)).astype(bf16)
    gv_ref[...] = mm_tn(probs.astype(bf16), grad).astype(bf16)
    soft = 1.0 / math.sqrt(HD)
    back_sine = -sin_ref[...]
    grad_q = turn(dot_nn(grad_scores, key) * soft, cos_ref[...], back_sine)
    grad_k = turn(mm_tn(grad_scores, query) * soft, cos_ref[...], back_sine)
    yq_ref[...] = grad_q
    yk_ref[...] = grad_k
    part_q = grad_q * raw_q
    part_k = grad_k * raw_k
    gains_ref[0:1, :] = jnp.sum(part_q * scale[:, 0:1], 0, keepdims=True)
    gains_ref[1:2, :] = jnp.sum(part_k * scale[:, 1:2], 0, keepdims=True)
    dot_q = jnp.sum(part_q * gains[0:1, :], -1, keepdims=True)
    dot_k = jnp.sum(part_k * gains[1:2, :], -1, keepdims=True)

    @pl.when(pl.program_id(0) == 0)
    def _():
        dots_ref[...] = jnp.zeros_like(dots_ref)

    column = lax.broadcasted_iota(jnp.int32, dots_ref.shape, 1)
    dots_ref[...] += jnp.where(column == 0, dot_q, dot_k)


def head_specs(seq, heads):
    one = pl.BlockSpec((seq, HD), lambda h: (0, h))
    key = pl.BlockSpec((seq, HD), lambda h: (0, heads + h))
    value = pl.BlockSpec((seq, HD), lambda h: (0, 2 * heads + h))

    def fixed(shape):
        return pl.BlockSpec(shape, lambda h: (0, 0))

    specs = [
        one,
        key,
        value,
        fixed((seq, 2)),
        pl.BlockSpec((2, HD), lambda h: (0, h)),
        fixed((seq, HD)),
        fixed((seq, HD)),
        fixed((seq, 1)),
        fixed((1, seq)),
    ]
    return one, specs


def attend(raw_qkv, tables):
    seq = raw_qkv.shape[0]
    width = raw_qkv.shape[1] // 3
    heads = width // HD
    one, specs = head_specs(seq, heads)
    return pl.pallas_call(
        attend_kernel,
        grid=(heads,),
        in_specs=specs,
        out_specs=one,
        out_shape=jax.ShapeDtypeStruct((seq, width), bf16),
        compiler_params=pltpu.CompilerParams(vmem_limit_bytes=48 << 20),
        cost_estimate=pl.CostEstimate(
            flops=4 * seq * seq * width,
            bytes_accessed=12 * seq * width,
            transcendentals=seq * seq * heads,
        ),
        name="attend",
    )(raw_qkv, raw_qkv, raw_qkv, *tables)


def attend_back(raw_qkv, tables, grad):
    seq, width = grad.shape
    heads = width // HD
    one, specs = head_specs(seq, heads)
    return pl.pallas_call(
        attend_back_kernel,
        grid=(heads,),
        in_specs=specs + [one],
        out_specs=[
            one,
            one,
            one,
            pl.BlockSpec((seq, 2), lambda h: (0, 0)),
            pl.BlockSpec((2, HD), lambda h: (0, h)),
        ],
        out_shape=[
            jax.ShapeDtypeStruct((seq, width), f32),
            jax.ShapeDtypeStruct((seq, width), f32),
            jax.ShapeDtypeStruct((seq, width), bf16),
            jax.ShapeDtypeStruct((seq, 2), f32),
            jax.ShapeDtypeStruct((2, width), f32),
        ],
        compiler_params=pltpu.CompilerParams(vmem_limit_bytes=56 << 20),
        cost_estimate=pl.CostEstimate(
            flops=12 * seq * seq * width,
            bytes_accessed=24 * seq * width,
            transcendentals=seq * seq * heads,
        ),
        name="attend_back",
    )(raw_qkv, raw_qkv, raw_qkv, *tables, grad)


def layer(
    tokens,
    attn_gain,
    query_gain,
    key_gain,
    w_query,
    w_key,
    w_value,
    output_weight,
    ffn_gain,
    router,
    experts,
    routes,
    cotangent,
):
    row_total = tokens.shape[1]
    half_rows = row_total // 2
    model_width = tokens.shape[2]
    expert_total = router.shape[1]
    slice_rows = experts.shape[0]
    local_experts = experts.shape[1]
    top_count = routes.shape[2]
    ff = experts.shape[2] // 3
    C = lax.axis_size("ctx")
    F = lax.axis_size("fsdp")
    devices = C * F
    W = model_width // C
    seq = C * row_total
    shard = w_query.shape[0]
    pieces = C // local_experts
    cap_unit = 16 * expert_total * pieces
    piece_cap = (17 * row_total * top_count + cap_unit - 1) // cap_unit
    me = lax.axis_index("ctx")
    row = lax.axis_index("fsdp")
    my_expert = row * local_experts + me // pieces
    my_column = me * W

    tokens_low = tokens.reshape(row_total, model_width)
    tokens_seq = gather_rows(tokens_low, C)
    route_ids = routes.reshape(row_total, top_count)
    column_ids = lax.all_gather(route_ids, "fsdp", axis=0, tiled=True)

    def by_column(weight):
        return jnp.swapaxes(weight.reshape(shard, C, W), 0, 1)

    w_cols = lax.all_to_all(
        jnp.concatenate([by_column(w_query), by_column(w_key), by_column(w_value)], 2),
        "ctx",
        split_axis=0,
        concat_axis=0,
        tiled=True,
    )
    w_qkv = lax.all_gather(w_cols, "fsdp", axis=1, tiled=True).reshape(model_width, 3 * W)
    w_o = lax.all_gather(output_weight, "fsdp", axis=0, tiled=True)

    by_expert = lax.optimization_barrier(
        jnp.swapaxes(lax.optimization_barrier(experts), 0, 1)
    )
    half = slice_rows // 2
    own = []
    order = []
    for j in range(C):
        for part in range(2):
            piece = lax.dynamic_slice(
                by_expert, ((me ^ j) // pieces, part * half, 0), (1, half, 3 * ff)
            ).reshape(half, 3 * ff)
            order.append((j, part))
            if j == 0:
                own.append(piece)
            else:
                own.append(from_peer(piece, j, C))
    expert = place_parts(me.reshape(1), order, own)

    column_rows = F * row_total
    member = jnp.sum(
        (column_ids[:, :, None] == jnp.arange(expert_total, dtype=jnp.int32)).astype(f32), 1
    )
    order = jnp.arange(row_total, dtype=jnp.int32)
    earlier = jnp.einsum(
        "ts,fse->fte",
        (order[None, :] < order[:, None]).astype(bf16),
        member.astype(bf16).reshape(F, row_total, expert_total),
        preferred_element_type=f32,
    ).reshape(column_rows, expert_total)
    marked = jnp.where(member > 0.5, earlier, -1.0).T
    group_rows = F * piece_cap
    group_ids = jnp.arange(group_rows, dtype=jnp.int32)
    token_block = jnp.arange(column_rows, dtype=jnp.int32) // row_total
    same_block = (group_ids // piece_cap)[:, None] == token_block[None, :]
    selects = []
    places = []
    for j in range(C):
        target = me ^ j
        mark = lax.dynamic_slice_in_dim(marked, row * local_experts + target // pieces, 1, 0)
        slot = (target % pieces) * piece_cap + group_ids % piece_cap
        slot = slot.astype(f32)
        selects.append(((mark == slot[:, None]) & same_block).astype(bf16))
        places.append(((mark.T == slot[None, :]) & same_block.T).astype(bf16))

    def exchange(parts):
        result = []
        for j in range(C):
            if j == 0:
                result.append(parts[j])
            else:
                result.append(from_peer(parts[j], j, C))
        return result

    def deliver(values):
        return exchange([mm(select, values).astype(bf16) for select in selects])

    def collect(parts):
        return collect_rows(places, parts)

    cot_low = cotangent.reshape(row_total, model_width)
    cot_column = lax.all_gather(cot_low, "fsdp", axis=0, tiled=True)
    cot_rows = deliver(cot_column)

    place = me ^ jnp.arange(C, dtype=jnp.int32)
    within = jnp.arange(half_rows, dtype=jnp.int32)
    positions = jnp.concatenate(
        [
            place[:, None] * half_rows + within,
            (2 * C - 1 - place)[:, None] * half_rows + within,
        ],
        1,
    ).reshape(seq)
    cosine, sine = rope_tables(positions, HD)
    inputs_seq = tokens_seq.astype(f32)
    scale_one = inv_rms(inputs_seq)
    normed = (inputs_seq * scale_one * attn_gain).astype(bf16)
    gains = lax.dynamic_slice_in_dim(jnp.stack([query_gain, key_gain]), my_column, W, 1)
    w_qkv, selects, places = lax.optimization_barrier((w_qkv, selects, places))
    raw_qkv = mm(normed, w_qkv)
    raw_q = raw_qkv[:, :W]
    raw_k = raw_qkv[:, W : 2 * W]
    squares = sum_rows(jnp.stack([jnp.sum(raw_q * raw_q, -1), jnp.sum(raw_k * raw_k, -1)]), C)
    scales = lax.rsqrt(squares / model_width + epsilon).T
    signed_sine = jnp.where(jnp.arange(HD) < HD // 2, -1.0, 1.0) * sine
    tables = (
        scales,
        gains,
        cosine,
        signed_sine,
        positions.reshape(seq, 1),
        positions.reshape(1, seq),
    )
    attended = attend(raw_qkv, tables)
    inputs = tokens_low.astype(f32)
    hidden_one = inputs + scatter_rows(mm(attended, w_o), C)

    scale_two = inv_rms(hidden_one)
    ffn_in = (hidden_one * scale_two * ffn_gain).astype(bf16)
    probs = jax.nn.softmax(mm(ffn_in, router), -1)
    ffn_column = lax.all_gather(ffn_in, "fsdp", axis=0, tiled=True)
    expert_in = deliver(ffn_column)
    extra = -(-2 * expert_total // 128) * 128
    done = []
    mine = my_expert.reshape(1)
    for j in range(C):
        result = run_expert(mine, expert_in[j], cot_rows[j], router, expert, extra)
        if j == 0:
            result, mine = lax.optimization_barrier((result, mine))
        done.append(result)
    back = collect(exchange([d[0] for d in done]))
    back = lax.psum_scatter(back, "fsdp", scatter_dimension=0, tiled=True).astype(f32)
    groups = [(expert_in[j], done[j][2], done[j][3], done[j][4], done[j][5]) for j in range(C)]
    d_own = []
    for j in range(C):
        d_own.append(weight_grad((me ^ j).reshape(1), groups, slice_rows))
    d_experts = None
    for part in range(2):
        pieces_here = []
        for j in range(C):
            if j == 0:
                pieces_here.append(d_own[j][part])
            else:
                pieces_here.append(from_peer(d_own[j][part], j, C))
        d_experts = merge_parts(
            (me // pieces).reshape(1),
            pieces_here,
            local_experts,
            part * half,
            slice_rows,
            d_experts,
        )
    mixed = collect(exchange([d[1] for d in done]))
    mixed = lax.psum_scatter(mixed, "fsdp", scatter_dimension=0, tiled=True).astype(f32)

    grad_probs = (
        back[:, model_width : model_width + expert_total]
        + back[:, model_width + expert_total : model_width + 2 * expert_total]
    )
    grad_logits = (probs * (grad_probs - jnp.sum(probs * grad_probs, -1, keepdims=True))).astype(
        bf16
    )
    grad_ffn = back[:, :model_width] + mm_nt(grad_logits, router)
    grad_router = mm_tn(grad_logits, ffn_in)
    grad_hidden_one, grad_ffn_gain = norm_back(grad_ffn, hidden_one, scale_two, ffn_gain)
    grad_hidden_one = grad_hidden_one + cot_low.astype(f32)
    router_slice = jnp.sum(
        lax.all_to_all(grad_router.reshape(devices, -1, 128), everyone, 0, 0, tiled=True), 0
    )

    branch_seq = gather_rows(grad_hidden_one.astype(bf16), C)
    d_output = mm_tn(attended, branch_seq).astype(bf16)
    grad_att = mm_nt(branch_seq, w_o).astype(bf16)
    grad_att, d_output = lax.optimization_barrier((grad_att, d_output))
    d_output = lax.psum_scatter(
        d_output, "fsdp", scatter_dimension=0, tiled=True
    ).astype(f32)
    grad_q_n, grad_k_n, grad_value, dots, gain_grads = attend_back(
        raw_qkv, tables, grad_att
    )
    dots = sum_rows(dots.T, C)
    dots = dots / model_width
    late_hidden, _ = lax.optimization_barrier((hidden_one, dots))
    output = (late_hidden + mixed).astype(bf16).reshape(1, row_total, model_width)
    scale_q = scales[:, 0:1]
    scale_k = scales[:, 1:2]
    grad_q = (
        scale_q * grad_q_n * gains[0]
        - raw_qkv[:, :W] * scale_q * scale_q * scale_q * dots[0][:, None]
    ).astype(bf16)
    grad_k = (
        scale_k * grad_k_n * gains[1]
        - raw_qkv[:, W : 2 * W] * scale_k * scale_k * scale_k * dots[1][:, None]
    ).astype(bf16)
    grad_qkv = jnp.concatenate([grad_q, grad_k, grad_value], 1)
    d_cols = lax.psum_scatter(
        mm_tn(normed, grad_qkv).astype(bf16).reshape(C, F * shard, 3 * W),
        "fsdp",
        scatter_dimension=1,
        tiled=True,
    )
    d_cols = lax.all_to_all(d_cols, "ctx", 0, 0, tiled=True).reshape(C, shard, 3, W)
    d_qkv = [
        jnp.swapaxes(d_cols[:, :, n], 0, 1).reshape(shard, model_width).astype(f32)
        for n in range(3)
    ]

    grad_normed = scatter_rows(mm_nt(grad_qkv, w_qkv), C)
    grad_inputs, grad_attn_gain = norm_back(grad_normed, inputs, scale_one[:row_total], attn_gain)
    grad_inputs = grad_inputs + grad_hidden_one

    vector = jnp.concatenate(
        [
            grad_attn_gain,
            grad_ffn_gain,
            gain_grads[0],
            gain_grads[1],
            router_slice.reshape(-1),
        ]
    ).reshape(1, -1, 128)
    everything = lax.all_to_all(
        jnp.broadcast_to(vector, (devices,) + vector.shape[1:]), everyone, 0, 0, tiled=True
    ).reshape(devices, -1)
    d_attn_gain = jnp.sum(everything[:, :model_width], 0)
    d_ffn_gain = jnp.sum(everything[:, model_width : 2 * model_width], 0)
    by_place = jnp.sum(
        everything[:, 2 * model_width : 2 * model_width + 2 * W].reshape(F, C, 2, W), 0
    )
    d_query_gain = by_place[:, 0].reshape(model_width)
    d_key_gain = by_place[:, 1].reshape(model_width)
    d_router = everything[:, 2 * model_width + 2 * W :].reshape(expert_total, model_width).T

    return (
        output,
        grad_inputs.reshape(1, row_total, model_width),
        d_attn_gain,
        d_query_gain,
        d_key_gain,
        d_qkv[0],
        d_qkv[1],
        d_qkv[2],
        d_output,
        d_ffn_gain,
        d_router,
        d_experts,
    )


def solution(mesh):
    placed = (
        P("fsdp", "ctx", None),
        P(),
        P(),
        P(),
        P(("ctx", "fsdp"), None),
        P(("ctx", "fsdp"), None),
        P(("ctx", "fsdp"), None),
        P(("ctx", "fsdp"), None),
        P(),
        P(),
        P("ctx", "fsdp", None),
        P("fsdp", "ctx", None),
        P("fsdp", "ctx", None),
    )
    return jax.shard_map(
        layer,
        mesh=mesh,
        in_specs=placed,
        out_specs=(
            P("fsdp", "ctx", None),
            P("fsdp", "ctx", None),
            P(),
            P(),
            P(),
            P(("ctx", "fsdp"), None),
            P(("ctx", "fsdp"), None),
            P(("ctx", "fsdp"), None),
            P(("ctx", "fsdp"), None),
            P(),
            P(),
            P("ctx", "fsdp", None),
        ),
        check_vma=False,
    )
```

```python
import functools
import math

import jax
import jax.numpy as jnp
from jax import lax
from jax.experimental import pallas as pl
from jax.experimental.pallas import tpu as pltpu
from jax.sharding import PartitionSpec as P

HD = 128

epsilon = 1e-05
neg_large = -1e30
f32 = jnp.float32
bf16 = jnp.bfloat16
everyone = ("fsdp", "ctx")


def mm(a, b):
    return jnp.dot(a, b, preferred_element_type=f32)


def mm_nt(a, b):
    return lax.dot_general(a, b, (((1,), (1,)), ((), ())), preferred_element_type=f32)


def mm_tn(a, b):
    return lax.dot_general(a, b, (((0,), (0,)), ((), ())), preferred_element_type=f32)


def inv_rms(values):
    return lax.rsqrt(jnp.mean(values * values, -1, keepdims=True) + epsilon)


def norm_back(grad, values, scale, gain):
    weighted = grad * gain
    grad_values = scale * weighted - values * scale * scale * scale * jnp.mean(
        weighted * values, -1, keepdims=True
    )
    grad_gain = jnp.sum(grad * values * scale, axis=0)
    return (grad_values, grad_gain)


def rope_tables(positions, head_size):
    half_size = head_size // 2
    inverse_freq = jnp.exp(
        jnp.arange(half_size, dtype=f32) * (-2.0 * math.log(10000.0) / head_size)
    )
    angles = positions.astype(f32)[:, None] * inverse_freq[None, :]
    cosine = jnp.cos(angles)
    sine = jnp.sin(angles)
    return (jnp.concatenate([cosine, cosine], -1), jnp.concatenate([sine, sine], -1))


def from_peer(values, offset, total):
    return lax.ppermute(values, "ctx", [(i, i ^ offset) for i in range(total)])


def place_kernel(order, rows, block, place_ref, *refs):
    parts, whole, sems = refs[:-2], refs[-2], refs[-1]
    step = pl.program_id(0)
    copies = []
    for n, (j, half) in enumerate(order):
        first = ((place_ref[0] ^ j) * 2 + half) * rows + step * block
        first = pl.multiple_of(first, block)
        copies.append(
            pltpu.make_async_copy(parts[n], whole.at[pl.ds(first, block), :], sems.at[n])
        )
        copies[-1].start()
    for copy in copies:
        copy.wait()


def place_parts(place, order, parts):
    rows, width = parts[0].shape
    block = min(64, rows)
    steps = rows // block
    return pl.pallas_call(
        functools.partial(place_kernel, order, rows, block),
        grid_spec=pltpu.PrefetchScalarGridSpec(
            num_scalar_prefetch=1,
            grid=(steps,),
            in_specs=[pl.BlockSpec((block, width), lambda i, s: (i, 0))] * len(parts),
            out_specs=pl.BlockSpec(memory_space=pl.ANY),
            scratch_shapes=[pltpu.SemaphoreType.DMA((len(parts),))],
        ),
        out_shape=jax.ShapeDtypeStruct((len(parts) * rows, width), parts[0].dtype),
        compiler_params=pltpu.CompilerParams(vmem_limit_bytes=30 << 20),
        cost_estimate=pl.CostEstimate(
            flops=0, bytes_accessed=4 * len(parts) * rows * width, transcendentals=0
        ),
        name="place_parts",
    )(place, *parts)


def merge_kernel(steps, block, total, pieces, base, place_ref, *refs):
    parts, whole, held, sems = refs[: total * pieces], refs[-3], refs[-2], refs[-1]
    step = pl.program_id(0)
    slot = lax.rem(step, 2)

    def copy(at, side, m):
        rows = pl.ds(pl.multiple_of(base + at * block, block), block)
        return pltpu.make_async_copy(
            held.at[side, m], whole.at[rows, place_ref[0] ^ m, :], sems.at[side, m]
        )

    for m in range(total):

        @pl.when(step >= 2)
        def _():
            copy(step - 2, slot, m).wait()

        value = parts[m * pieces][...].astype(f32)
        for p in range(1, pieces):
            value = value + parts[m * pieces + p][...].astype(f32)
        held[slot, m] = value
        copy(step, slot, m).start()

    @pl.when(step == steps - 1)
    def _():
        for m in range(total):
            if steps >= 2:
                copy(step - 1, 1 - slot, m).wait()
            copy(step, slot, m).wait()


def merge_parts(place, parts, total, base, rows_total, whole=None):
    rows, width = parts[0].shape
    pieces = len(parts) // total
    block = min(64, rows)
    steps = rows // block
    more = [] if whole is None else [whole]
    return pl.pallas_call(
        functools.partial(merge_kernel, steps, block, total, pieces, base),
        grid_spec=pltpu.PrefetchScalarGridSpec(
            num_scalar_prefetch=1,
            grid=(steps,),
            in_specs=[pl.BlockSpec((block, width), lambda i, s: (i, 0))] * len(parts)
            + [pl.BlockSpec(memory_space=pl.ANY)] * len(more),
            out_specs=pl.BlockSpec(memory_space=pl.ANY),
            scratch_shapes=[
                pltpu.VMEM((2, total, block, width), f32),
                pltpu.SemaphoreType.DMA((2, total)),
            ],
        ),
        out_shape=jax.ShapeDtypeStruct((rows_total, total, width), f32),
        input_output_aliases={1 + len(parts): 0} if more else {},
        compiler_params=pltpu.CompilerParams(vmem_limit_bytes=30 << 20),
        cost_estimate=pl.CostEstimate(
            flops=0,
            bytes_accessed=2 * len(parts) * rows * width + 4 * total * rows * width,
            transcendentals=0,
        ),
        name="merge_parts",
    )(place, *parts, *more)


def gather_rows(values, total):
    return jnp.concatenate(
        [values] + [from_peer(values, j, total) for j in range(1, total)], 0
    )


def scatter_rows(partial, total):
    rows = partial.shape[0] // total
    result = partial[:rows]
    for j in range(1, total):
        piece = partial[j * rows : (j + 1) * rows].astype(bf16)
        result = result + from_peer(piece, j, total).astype(f32)
    return result


def spread_rows(values, total):
    return [values] + [from_peer(values, j, total) for j in range(1, total)]


def add_rows(refs):
    total = len(refs)
    result = refs[0][...]
    rows = result.shape[1] // total
    for j in range(1, total):
        other = refs[j][...]
        blocks = [other[:, (i ^ j) * rows : ((i ^ j) + 1) * rows] for i in range(total)]
        result = result + jnp.concatenate(blocks, 1)
    return result


def diagonal(size):
    first = lax.broadcasted_iota(jnp.int32, (size, size), 0)
    return first == lax.broadcasted_iota(jnp.int32, (size, size), 1)


def as_column(row):
    return jnp.sum(jnp.where(diagonal(row.shape[1]), row, 0.0), 1, keepdims=True)


def as_row(column):
    return jnp.sum(jnp.where(diagonal(column.shape[0]), column, 0.0), 0, keepdims=True)


def dot_nn(a, b):
    return lax.dot_general(a, b, (((1,), (0,)), ((), ())), preferred_element_type=f32)


def expert_kernel(
    steps,
    mine_ref,
    rows_ref,
    cots_ref,
    router_ref,
    gate_w,
    up_w,
    down_w,
    back_ref,
    out_ref,
    grads_ref,
    ggate_ref,
    gup_ref,
    hidden_ref,
    total_out,
    total_back,
    weight,
):
    step = pl.program_id(0)
    mine = mine_ref[0]
    width = rows_ref.shape[1]
    expert_total = router_ref.shape[1]

    @pl.when(step == 0)
    def _():
        logits = dot_nn(rows_ref[...], router_ref[...])
        logits = jnp.exp(logits - jnp.max(logits, -1, keepdims=True))
        column = lax.broadcasted_iota(jnp.int32, logits.shape, 1)
        chosen = jnp.sum(jnp.where(column == mine, logits, 0.0), -1, keepdims=True)
        weight[...] = chosen / jnp.sum(logits, -1, keepdims=True)
        grads_ref[...] = (weight[...] * cots_ref[...].astype(f32)).astype(bf16)
        total_out[...] = jnp.zeros_like(total_out)
        total_back[...] = jnp.zeros_like(total_back)

    gate = dot_nn(rows_ref[...], gate_w[...])
    up = dot_nn(rows_ref[...], up_w[...])
    grad_hidden = dot_nn(grads_ref[...], down_w[...])
    sigma = jax.nn.sigmoid(gate)
    swish = gate * sigma
    hidden = (swish * up).astype(bf16)
    grad_gate = (grad_hidden * up * sigma * (1.0 + gate * (1.0 - sigma))).astype(bf16)
    grad_up = (grad_hidden * swish).astype(bf16)
    hidden_ref[...] = hidden
    ggate_ref[...] = grad_gate
    gup_ref[...] = grad_up
    total_out[...] += mm_nt(hidden, down_w[...])
    total_back[...] += mm_nt(grad_gate, gate_w[...]) + mm_nt(grad_up, up_w[...])

    @pl.when(step == steps - 1)
    def _():
        result = total_out[...].astype(bf16).astype(f32)
        out_ref[...] = (weight[...] * result).astype(bf16)
        grad_weight = jnp.sum(cots_ref[...].astype(f32) * result, -1, keepdims=True)
        high = grad_weight.astype(bf16).astype(f32)
        low = grad_weight - high
        back_ref[:, :width] = total_back[...].astype(bf16)
        extra = back_ref.shape[1] - width
        column = lax.broadcasted_iota(jnp.int32, (rows_ref.shape[0], extra), 1)
        side = jnp.where(column == mine, high, 0.0) + jnp.where(
            column == expert_total + mine, low, 0.0
        )
        back_ref[:, width:] = side.astype(bf16)


def run_expert(mine, rows, cots, router, expert, extra):
    count, width = rows.shape
    ff = expert.shape[1] // 3
    block = min(256, ff)
    steps = ff // block
    whole = pl.BlockSpec((count, width), lambda i, s: (0, 0))
    part = pl.BlockSpec((count, block), lambda i, s: (0, i))
    return pl.pallas_call(
        functools.partial(expert_kernel, steps),
        grid_spec=pltpu.PrefetchScalarGridSpec(
            num_scalar_prefetch=1,
            grid=(steps,),
            in_specs=[
                whole,
                whole,
                pl.BlockSpec(router.shape, lambda i, s: (0, 0)),
                pl.BlockSpec((width, block), lambda i, s: (0, i)),
                pl.BlockSpec((width, block), lambda i, s: (0, steps + i)),
                pl.BlockSpec((width, block), lambda i, s: (0, 2 * steps + i)),
            ],
            out_specs=[
                pl.BlockSpec((count, width + extra), lambda i, s: (0, 0)),
                whole,
                whole,
                part,
                part,
                part,
            ],
            scratch_shapes=[
                pltpu.VMEM((count, width), f32),
                pltpu.VMEM((count, width), f32),
                pltpu.VMEM((count, 1), f32),
            ],
        ),
        out_shape=[
            jax.ShapeDtypeStruct((count, width + extra), bf16),
            jax.ShapeDtypeStruct((count, width), bf16),
            jax.ShapeDtypeStruct((count, width), bf16),
            jax.ShapeDtypeStruct((count, ff), bf16),
            jax.ShapeDtypeStruct((count, ff), bf16),
            jax.ShapeDtypeStruct((count, ff), bf16),
        ],
        compiler_params=pltpu.CompilerParams(vmem_limit_bytes=48 << 20),
        cost_estimate=pl.CostEstimate(
            flops=12 * count * width * ff,
            bytes_accessed=6 * width * ff + 10 * count * width,
            transcendentals=count * ff,
        ),
        name="expert",
    )(mine, rows, cots, router, expert, expert, expert)


def weight_kernel(groups, steps, place_ref, *refs):
    step = pl.program_id(0)

    def total(left, right):
        result = mm_tn(refs[left][...], refs[right][...])
        for g in range(1, groups):
            result = result + mm_tn(refs[5 * g + left][...], refs[5 * g + right][...])
        half = refs[-1].shape[0]
        refs[-2][...] = result[:half].astype(bf16)
        refs[-1][...] = result[half:].astype(bf16)

    @pl.when(step < steps)
    def _():
        total(0, 2)

    @pl.when((step >= steps) & (step < 2 * steps))
    def _():
        total(0, 3)

    @pl.when(step >= 2 * steps)
    def _():
        total(1, 4)


def weight_grad(place, groups, columns):
    count, _ = groups[0][0].shape
    ff = groups[0][2].shape[1]
    block = min(512, ff)
    steps = ff // block
    side = pl.BlockSpec((count, columns), lambda i, s: (0, s[0]))

    def part(first):
        return pl.BlockSpec(
            (count, block),
            lambda i, s: (0, jnp.clip(i - first * steps, 0, steps - 1)),
        )

    return pl.pallas_call(
        functools.partial(weight_kernel, len(groups), steps),
        grid_spec=pltpu.PrefetchScalarGridSpec(
            num_scalar_prefetch=1,
            grid=(3 * steps,),
            in_specs=[side, side, part(0), part(1), part(2)] * len(groups),
            out_specs=[pl.BlockSpec((columns // 2, block), lambda i, s: (0, i))] * 2,
        ),
        out_shape=[jax.ShapeDtypeStruct((columns // 2, 3 * ff), bf16)] * 2,
        compiler_params=pltpu.CompilerParams(vmem_limit_bytes=48 << 20),
        cost_estimate=pl.CostEstimate(
            flops=6 * len(groups) * count * columns * ff,
            bytes_accessed=6 * columns * ff + 10 * len(groups) * count * ff,
            transcendentals=0,
        ),
        name="weight_grad",
    )(place, *[a for group in groups for a in group])


def collect_kernel(total, *refs):
    result = dot_nn(refs[0][...], refs[total][...])
    for j in range(1, total):
        result = result + dot_nn(refs[j][...], refs[total + j][...])
    refs[-1][...] = result.astype(bf16)


def collect_rows(places, parts):
    tokens = places[0].shape[0]
    rows, width = parts[0].shape
    block = 512 if width % 512 == 0 else 768
    return pl.pallas_call(
        functools.partial(collect_kernel, len(parts)),
        grid=(pl.cdiv(width, block),),
        in_specs=[pl.BlockSpec((tokens, rows), lambda i: (0, 0))] * len(parts)
        + [pl.BlockSpec((rows, block), lambda i: (0, i))] * len(parts),
        out_specs=pl.BlockSpec((tokens, block), lambda i: (0, i)),
        out_shape=jax.ShapeDtypeStruct((tokens, width), bf16),
        compiler_params=pltpu.CompilerParams(vmem_limit_bytes=48 << 20),
        cost_estimate=pl.CostEstimate(
            flops=2 * len(parts) * tokens * rows * width,
            bytes_accessed=2 * len(parts) * rows * (width + tokens) + 2 * tokens * width,
            transcendentals=0,
        ),
        name="collect_rows",
    )(*places, *parts)


def turn(values, cosine, sine):
    return values * cosine + pltpu.roll(values, HD // 2, 1) * sine


def head_forward(raw_q, raw_k, scale, gains, cosine, sine, row_pos, col_pos):
    query = turn(raw_q * scale[:, 0:1] * gains[0:1, :], cosine, sine).astype(bf16)
    key = turn(raw_k * scale[:, 1:2] * gains[1:2, :], cosine, sine).astype(bf16)
    scores = mm_nt(query, key) * (1.0 / math.sqrt(HD))
    scores = jnp.where(col_pos <= row_pos, scores, neg_large)
    weights = jnp.exp(scores - jnp.max(scores, -1, keepdims=True))
    return query, key, weights / jnp.sum(weights, -1, keepdims=True)


def attend_kernel(model_width, q_ref, k_ref, v_ref, gain_ref, cos_ref, sin_ref, rp, cp, *refs):
    parts, out_ref, scale_ref = refs[:-2], refs[-2], refs[-1]

    @pl.when(pl.program_id(0) == 0)
    def _():
        scale = lax.rsqrt(add_rows(parts) / model_width + epsilon)
        for n in range(2):
            scale_ref[:, n : n + 1] = as_column(scale[n : n + 1, :])

    _, _, probs = head_forward(
        q_ref[...],
        k_ref[...],
        scale_ref[...],
        gain_ref[...],
        cos_ref[...],
        sin_ref[...],
        rp[...],
        cp[...],
    )
    out_ref[...] = dot_nn(probs.astype(bf16), v_ref[...].astype(bf16)).astype(bf16)


def attend_back_kernel(
    q_ref,
    k_ref,
    v_ref,
    gain_ref,
    cos_ref,
    sin_ref,
    rp,
    cp,
    scale_ref,
    grad_ref,
    yq_ref,
    yk_ref,
    gv_ref,
    dots_ref,
    gains_ref,
    held,
):
    head = pl.program_id(0)
    raw_q = q_ref[...]
    raw_k = k_ref[...]
    scale = scale_ref[...]
    gains = gain_ref[...]
    query, key, probs = head_forward(
        raw_q, raw_k, scale, gains, cos_ref[...], sin_ref[...], rp[...], cp[...]
    )
    grad = grad_ref[...]
    grad_prob = mm_nt(grad, v_ref[...].astype(bf16))
    delta = jnp.sum(probs * grad_prob, -1, keepdims=True)
    grad_scores = (probs * (grad_prob - delta)).astype(bf16)
    gv_ref[...] = mm_tn(probs.astype(bf16), grad).astype(bf16)
    soft = 1.0 / math.sqrt(HD)
    back_sine = -sin_ref[...]
    grad_q = turn(dot_nn(grad_scores, key) * soft, cos_ref[...], back_sine)
    grad_k = turn(mm_tn(grad_scores, query) * soft, cos_ref[...], back_sine)
    yq_ref[...] = grad_q
    yk_ref[...] = grad_k
    part_q = grad_q * raw_q
    part_k = grad_k * raw_k
    gains_ref[0:1, :] = jnp.sum(part_q * scale[:, 0:1], 0, keepdims=True)
    gains_ref[1:2, :] = jnp.sum(part_k * scale[:, 1:2], 0, keepdims=True)
    dot_q = jnp.sum(part_q * gains[0:1, :], -1, keepdims=True)
    dot_k = jnp.sum(part_k * gains[1:2, :], -1, keepdims=True)

    @pl.when(head == 0)
    def _():
        held[...] = jnp.zeros_like(held)

    held[:, 0:1] += dot_q
    held[:, 1:2] += dot_k

    @pl.when(head == pl.num_programs(0) - 1)
    def _():
        for n in range(2):
            dots_ref[n : n + 1, :] = as_row(held[:, n : n + 1])


def finish_kernel(model_width, heads, yq_ref, yk_ref, gv_ref, raw_ref, gain_ref, scale_ref, *refs):
    parts, out_ref, dots = refs[:-2], refs[-2], refs[-1]
    step = pl.program_id(0)

    @pl.when(step == 0)
    def _():
        total = add_rows(parts) / model_width
        for n in range(2):
            dots[:, n : n + 1] = as_column(total[n : n + 1, :])

    def through(n, grad):
        scale = scale_ref[:, n : n + 1]
        cube = scale * scale * scale * dots[:, n : n + 1]
        out_ref[...] = (scale * (grad * gain_ref[n : n + 1, :]) - raw_ref[...] * cube).astype(bf16)

    @pl.when(step < heads)
    def _():
        through(0, yq_ref[...])

    @pl.when((step >= heads) & (step < 2 * heads))
    def _():
        through(1, yk_ref[...])

    @pl.when(step >= 2 * heads)
    def _():
        out_ref[...] = gv_ref[...]


def finish(model_width, yq, yk, gv, raw_qkv, gains, scales, parts):
    seq, width = gv.shape
    heads = width // HD

    def block(first, last):
        return pl.BlockSpec((seq, HD), lambda i: (0, jnp.clip(i - first, 0, last)))

    return pl.pallas_call(
        functools.partial(finish_kernel, model_width, heads),
        grid=(3 * heads,),
        in_specs=[
            block(0, heads - 1),
            block(heads, heads - 1),
            block(2 * heads, heads - 1),
            block(0, 2 * heads - 1),
            pl.BlockSpec((2, HD), lambda i: (0, lax.rem(i, heads))),
            pl.BlockSpec((seq, 2), lambda i: (0, 0)),
        ]
        + [pl.BlockSpec((2, seq), lambda i: (0, 0))] * len(parts),
        out_specs=pl.BlockSpec((seq, HD), lambda i: (0, i)),
        out_shape=jax.ShapeDtypeStruct((seq, 3 * width), bf16),
        scratch_shapes=[pltpu.VMEM((seq, 2), f32)],
        compiler_params=pltpu.CompilerParams(vmem_limit_bytes=48 << 20),
        cost_estimate=pl.CostEstimate(
            flops=16 * seq * width, bytes_accessed=26 * seq * width, transcendentals=0
        ),
        name="finish",
    )(yq, yk, gv, raw_qkv, gains, scales, *parts)


def head_specs(seq, heads):
    one = pl.BlockSpec((seq, HD), lambda h: (0, h))
    key = pl.BlockSpec((seq, HD), lambda h: (0, heads + h))
    value = pl.BlockSpec((seq, HD), lambda h: (0, 2 * heads + h))

    def fixed(shape):
        return pl.BlockSpec(shape, lambda h: (0, 0))

    specs = [
        one,
        key,
        value,
        pl.BlockSpec((2, HD), lambda h: (0, h)),
        fixed((seq, HD)),
        fixed((seq, HD)),
        fixed((seq, 1)),
        fixed((1, seq)),
    ]
    return one, specs, fixed


def attend(raw_qkv, tables, parts, model_width):
    seq = raw_qkv.shape[0]
    width = raw_qkv.shape[1] // 3
    heads = width // HD
    one, specs, fixed = head_specs(seq, heads)
    return pl.pallas_call(
        functools.partial(attend_kernel, model_width),
        grid=(heads,),
        in_specs=specs + [fixed((2, seq))] * len(parts),
        out_specs=[one, fixed((seq, 2))],
        out_shape=[
            jax.ShapeDtypeStruct((seq, width), bf16),
            jax.ShapeDtypeStruct((seq, 2), f32),
        ],
        compiler_params=pltpu.CompilerParams(vmem_limit_bytes=48 << 20),
        cost_estimate=pl.CostEstimate(
            flops=4 * seq * seq * width,
            bytes_accessed=12 * seq * width,
            transcendentals=seq * seq * heads,
        ),
        name="attend",
    )(raw_qkv, raw_qkv, raw_qkv, *tables, *parts)


def attend_back(raw_qkv, tables, scales, grad):
    seq, width = grad.shape
    heads = width // HD
    one, specs, fixed = head_specs(seq, heads)
    return pl.pallas_call(
        attend_back_kernel,
        grid=(heads,),
        in_specs=specs + [fixed((seq, 2)), one],
        out_specs=[one, one, one, fixed((2, seq)), pl.BlockSpec((2, HD), lambda h: (0, h))],
        out_shape=[
            jax.ShapeDtypeStruct((seq, width), f32),
            jax.ShapeDtypeStruct((seq, width), f32),
            jax.ShapeDtypeStruct((seq, width), bf16),
            jax.ShapeDtypeStruct((2, seq), f32),
            jax.ShapeDtypeStruct((2, width), f32),
        ],
        scratch_shapes=[pltpu.VMEM((seq, 2), f32)],
        compiler_params=pltpu.CompilerParams(vmem_limit_bytes=56 << 20),
        cost_estimate=pl.CostEstimate(
            flops=12 * seq * seq * width,
            bytes_accessed=24 * seq * width,
            transcendentals=seq * seq * heads,
        ),
        name="attend_back",
    )(raw_qkv, raw_qkv, raw_qkv, *tables, scales, grad)


def layer(
    tokens,
    attn_gain,
    query_gain,
    key_gain,
    w_query,
    w_key,
    w_value,
    output_weight,
    ffn_gain,
    router,
    experts,
    routes,
    cotangent,
):
    row_total = tokens.shape[1]
    half_rows = row_total // 2
    model_width = tokens.shape[2]
    expert_total = router.shape[1]
    slice_rows = experts.shape[0]
    local_experts = experts.shape[1]
    top_count = routes.shape[2]
    ff = experts.shape[2] // 3
    C = lax.axis_size("ctx")
    F = lax.axis_size("fsdp")
    devices = C * F
    W = model_width // C
    seq = C * row_total
    shard = w_query.shape[0]
    pieces = C // local_experts
    cap_unit = 16 * expert_total * pieces
    piece_cap = (17 * row_total * top_count + cap_unit - 1) // cap_unit
    me = lax.axis_index("ctx")
    row = lax.axis_index("fsdp")
    my_expert = row * local_experts + me // pieces
    my_column = me * W

    tokens_low = tokens.reshape(row_total, model_width)
    tokens_seq = gather_rows(tokens_low, C)
    route_ids = routes.reshape(row_total, top_count)
    column_ids = lax.all_gather(route_ids, "fsdp", axis=0, tiled=True)

    def by_column(weight):
        return jnp.swapaxes(weight.reshape(shard, C, W), 0, 1)

    w_cols = lax.all_to_all(
        jnp.concatenate([by_column(w_query), by_column(w_key), by_column(w_value)], 2),
        "ctx",
        split_axis=0,
        concat_axis=0,
        tiled=True,
    )
    w_qkv = lax.all_gather(w_cols, "fsdp", axis=1, tiled=True).reshape(model_width, 3 * W)
    w_o = lax.all_gather(output_weight, "fsdp", axis=0, tiled=True)

    by_expert = lax.optimization_barrier(
        jnp.swapaxes(lax.optimization_barrier(experts), 0, 1)
    )
    half = slice_rows // 2
    own = []
    order = []
    for j in range(C):
        for part in range(2):
            piece = lax.dynamic_slice(
                by_expert, ((me ^ j) // pieces, part * half, 0), (1, half, 3 * ff)
            ).reshape(half, 3 * ff)
            order.append((j, part))
            if j == 0:
                own.append(piece)
            else:
                own.append(from_peer(piece, j, C))
    expert = place_parts(me.reshape(1), order, own)

    column_rows = F * row_total
    member = jnp.sum(
        (column_ids[:, :, None] == jnp.arange(expert_total, dtype=jnp.int32)).astype(f32), 1
    )
    order = jnp.arange(row_total, dtype=jnp.int32)
    earlier = jnp.einsum(
        "ts,fse->fte",
        (order[None, :] < order[:, None]).astype(bf16),
        member.astype(bf16).reshape(F, row_total, expert_total),
        preferred_element_type=f32,
    ).reshape(column_rows, expert_total)
    marked = jnp.where(member > 0.5, earlier, -1.0).T
    group_rows = F * piece_cap
    group_ids = jnp.arange(group_rows, dtype=jnp.int32)
    token_block = jnp.arange(column_rows, dtype=jnp.int32) // row_total
    same_block = (group_ids // piece_cap)[:, None] == token_block[None, :]
    selects = []
    places = []
    for j in range(C):
        target = me ^ j
        mark = lax.dynamic_slice_in_dim(marked, row * local_experts + target // pieces, 1, 0)
        slot = (target % pieces) * piece_cap + group_ids % piece_cap
        slot = slot.astype(f32)
        selects.append(((mark == slot[:, None]) & same_block).astype(bf16))
        places.append(((mark.T == slot[None, :]) & same_block.T).astype(bf16))

    def exchange(parts):
        result = []
        for j in range(C):
            if j == 0:
                result.append(parts[j])
            else:
                result.append(from_peer(parts[j], j, C))
        return result

    def deliver(values):
        return exchange([mm(select, values).astype(bf16) for select in selects])

    def collect(parts):
        return collect_rows(places, parts)

    cot_low = cotangent.reshape(row_total, model_width)
    cot_column = lax.all_gather(cot_low, "fsdp", axis=0, tiled=True)
    cot_rows = deliver(cot_column)

    place = me ^ jnp.arange(C, dtype=jnp.int32)
    within = jnp.arange(half_rows, dtype=jnp.int32)
    positions = jnp.concatenate(
        [
            place[:, None] * half_rows + within,
            (2 * C - 1 - place)[:, None] * half_rows + within,
        ],
        1,
    ).reshape(seq)
    cosine, sine = rope_tables(positions, HD)
    inputs_seq = tokens_seq.astype(f32)
    scale_one = inv_rms(inputs_seq)
    normed = (inputs_seq * scale_one * attn_gain).astype(bf16)
    gains = lax.dynamic_slice_in_dim(jnp.stack([query_gain, key_gain]), my_column, W, 1)
    w_qkv, selects, places = lax.optimization_barrier((w_qkv, selects, places))
    raw_qkv = mm(normed, w_qkv)
    raw_q = raw_qkv[:, :W]
    raw_k = raw_qkv[:, W : 2 * W]
    squares = spread_rows(jnp.stack([jnp.sum(raw_q * raw_q, -1), jnp.sum(raw_k * raw_k, -1)]), C)
    signed_sine = jnp.where(jnp.arange(HD) < HD // 2, -1.0, 1.0) * sine
    tables = (gains, cosine, signed_sine, positions.reshape(seq, 1), positions.reshape(1, seq))
    attended, scales = attend(raw_qkv, tables, squares, model_width)
    inputs = tokens_low.astype(f32)
    hidden_one = inputs + scatter_rows(mm(attended, w_o), C)

    scale_two = inv_rms(hidden_one)
    ffn_in = (hidden_one * scale_two * ffn_gain).astype(bf16)
    probs = jax.nn.softmax(mm(ffn_in, router), -1)
    ffn_column = lax.all_gather(ffn_in, "fsdp", axis=0, tiled=True)
    expert_in = deliver(ffn_column)
    extra = -(-2 * expert_total // 128) * 128
    done = []
    mine = my_expert.reshape(1)
    for j in range(C):
        result = run_expert(mine, expert_in[j], cot_rows[j], router, expert, extra)
        if j == 0:
            result, mine = lax.optimization_barrier((result, mine))
        done.append(result)
    back = collect(exchange([d[0] for d in done]))
    back = lax.psum_scatter(back, "fsdp", scatter_dimension=0, tiled=True).astype(f32)
    groups = [(expert_in[j], done[j][2], done[j][3], done[j][4], done[j][5]) for j in range(C)]
    d_own = []
    for j in range(C):
        d_own.append(weight_grad((me ^ j).reshape(1), groups, slice_rows))
    d_experts = None
    for part in range(2):
        pieces_here = []
        for j in range(C):
            if j == 0:
                pieces_here.append(d_own[j][part])
            else:
                pieces_here.append(from_peer(d_own[j][part], j, C))
        d_experts = merge_parts(
            (me // pieces).reshape(1),
            pieces_here,
            local_experts,
            part * half,
            slice_rows,
            d_experts,
        )
    mixed = collect(exchange([d[1] for d in done]))
    mixed = lax.psum_scatter(mixed, "fsdp", scatter_dimension=0, tiled=True).astype(f32)

    grad_probs = (
        back[:, model_width : model_width + expert_total]
        + back[:, model_width + expert_total : model_width + 2 * expert_total]
    )
    grad_logits = (probs * (grad_probs - jnp.sum(probs * grad_probs, -1, keepdims=True))).astype(
        bf16
    )
    grad_ffn = back[:, :model_width] + mm_nt(grad_logits, router)
    grad_router = mm_tn(grad_logits, ffn_in)
    grad_hidden_one, grad_ffn_gain = norm_back(grad_ffn, hidden_one, scale_two, ffn_gain)
    grad_hidden_one = grad_hidden_one + cot_low.astype(f32)
    router_slice = jnp.sum(
        lax.all_to_all(grad_router.reshape(devices, -1, 128), everyone, 0, 0, tiled=True), 0
    )

    branch_seq = gather_rows(grad_hidden_one.astype(bf16), C)
    d_output = mm_tn(attended, branch_seq).astype(bf16)
    grad_att = mm_nt(branch_seq, w_o).astype(bf16)
    grad_att, d_output = lax.optimization_barrier((grad_att, d_output))
    d_output = lax.psum_scatter(
        d_output, "fsdp", scatter_dimension=0, tiled=True
    ).astype(f32)
    grad_q_n, grad_k_n, grad_value, dots, gain_grads = attend_back(
        raw_qkv, tables, scales, grad_att
    )
    dots = spread_rows(dots, C)
    late_hidden, dots = lax.optimization_barrier((hidden_one, dots))
    output = (late_hidden + mixed).astype(bf16).reshape(1, row_total, model_width)
    grad_qkv = finish(
        model_width, grad_q_n, grad_k_n, grad_value, raw_qkv, gains, scales, dots
    )
    d_cols = lax.psum_scatter(
        mm_tn(normed, grad_qkv).astype(bf16).reshape(C, F * shard, 3 * W),
        "fsdp",
        scatter_dimension=1,
        tiled=True,
    )
    d_cols = lax.all_to_all(d_cols, "ctx", 0, 0, tiled=True).reshape(C, shard, 3, W)
    d_qkv = [
        jnp.swapaxes(d_cols[:, :, n], 0, 1).reshape(shard, model_width).astype(f32)
        for n in range(3)
    ]

    grad_normed = scatter_rows(mm_nt(grad_qkv, w_qkv), C)
    grad_inputs, grad_attn_gain = norm_back(grad_normed, inputs, scale_one[:row_total], attn_gain)
    grad_inputs = grad_inputs + grad_hidden_one

    vector = jnp.concatenate(
        [
            grad_attn_gain,
            grad_ffn_gain,
            gain_grads[0],
            gain_grads[1],
            router_slice.reshape(-1),
        ]
    ).reshape(1, -1, 128)
    everything = lax.all_to_all(
        jnp.broadcast_to(vector, (devices,) + vector.shape[1:]), everyone, 0, 0, tiled=True
    ).reshape(devices, -1)
    d_attn_gain = jnp.sum(everything[:, :model_width], 0)
    d_ffn_gain = jnp.sum(everything[:, model_width : 2 * model_width], 0)
    by_place = jnp.sum(
        everything[:, 2 * model_width : 2 * model_width + 2 * W].reshape(F, C, 2, W), 0
    )
    d_query_gain = by_place[:, 0].reshape(model_width)
    d_key_gain = by_place[:, 1].reshape(model_width)
    d_router = everything[:, 2 * model_width + 2 * W :].reshape(expert_total, model_width).T

    return (
        output,
        grad_inputs.reshape(1, row_total, model_width),
        d_attn_gain,
        d_query_gain,
        d_key_gain,
        d_qkv[0],
        d_qkv[1],
        d_qkv[2],
        d_output,
        d_ffn_gain,
        d_router,
        d_experts,
    )


def solution(mesh):
    placed = (
        P("fsdp", "ctx", None),
        P(),
        P(),
        P(),
        P(("ctx", "fsdp"), None),
        P(("ctx", "fsdp"), None),
        P(("ctx", "fsdp"), None),
        P(("ctx", "fsdp"), None),
        P(),
        P(),
        P("ctx", "fsdp", None),
        P("fsdp", "ctx", None),
        P("fsdp", "ctx", None),
    )
    return jax.shard_map(
        layer,
        mesh=mesh,
        in_specs=placed,
        out_specs=(
            P("fsdp", "ctx", None),
            P("fsdp", "ctx", None),
            P(),
            P(),
            P(),
            P(("ctx", "fsdp"), None),
            P(("ctx", "fsdp"), None),
            P(("ctx", "fsdp"), None),
            P(("ctx", "fsdp"), None),
            P(),
            P(),
            P("ctx", "fsdp", None),
        ),
        check_vma=False,
    )
```

```python
import functools
import math

import jax
import jax.numpy as jnp
from jax import lax
from jax.experimental import pallas as pl
from jax.experimental.pallas import tpu as pltpu
from jax.sharding import PartitionSpec as P

HD = 128

epsilon = 1e-05
neg_large = -1e30
f32 = jnp.float32
bf16 = jnp.bfloat16
CTX = "ctx"
FSDP = "fsdp"
everyone = (FSDP, CTX)


def mm(a, b):
    return jnp.dot(a, b, preferred_element_type=f32)


def mm_nt(a, b):
    return lax.dot_general(a, b, (((1,), (1,)), ((), ())), preferred_element_type=f32)


def mm_tn(a, b):
    return lax.dot_general(a, b, (((0,), (0,)), ((), ())), preferred_element_type=f32)


def inv_rms(values):
    return lax.rsqrt(jnp.mean(values * values, -1, keepdims=True) + epsilon)


def norm_back(grad, values, scale, gain):
    weighted = grad * gain
    grad_values = scale * weighted - values * scale * scale * scale * jnp.mean(
        weighted * values, -1, keepdims=True
    )
    grad_gain = jnp.sum(grad * values * scale, axis=0)
    return (grad_values, grad_gain)


def rope_tables(positions, head_size):
    half_size = head_size // 2
    inverse_freq = jnp.exp(
        jnp.arange(half_size, dtype=f32) * (-2.0 * math.log(10000.0) / head_size)
    )
    angles = positions.astype(f32)[:, None] * inverse_freq[None, :]
    cosine = jnp.cos(angles)
    sine = jnp.sin(angles)
    return (jnp.concatenate([cosine, cosine], -1), jnp.concatenate([sine, sine], -1))


def from_peer(values, offset, total):
    return lax.ppermute(values, CTX, [(i, i ^ offset) for i in range(total)])


def place_kernel(order, total, place_ref, *refs):
    parts, whole, sems = refs[:-2], refs[-2], refs[-1]
    step = pl.program_id(0)

    def copy(n):
        j, begin, rows = order[n]
        block = min(64, rows)
        first = pl.multiple_of((place_ref[0] ^ j) * total + begin + step * block, block)
        part = parts[n].at[0] if j == 0 else parts[n]
        return pltpu.make_async_copy(part, whole.at[pl.ds(first, block), :], sems.at[n])

    for n in range(len(parts)):

        @pl.when(step < order[n][2] // min(64, order[n][2]))
        def _():
            copy(n).start()

    for n in range(len(parts)):

        @pl.when(step < order[n][2] // min(64, order[n][2]))
        def _():
            copy(n).wait()


def place_parts(place, pieces, order, parts, total):
    width = parts[0].shape[-1]
    places = max(o[0] for o in order) + 1

    def spec(j, begin, rows):
        block = min(64, rows)
        last = rows // block - 1
        if j == 0:
            return pl.BlockSpec(
                (1, block, width),
                lambda i, s: (s[0] // pieces, begin // block + jnp.minimum(i, last), 0),
            )
        return pl.BlockSpec((block, width), lambda i, s: (jnp.minimum(i, last), 0))

    return pl.pallas_call(
        functools.partial(place_kernel, order, total),
        grid_spec=pltpu.PrefetchScalarGridSpec(
            num_scalar_prefetch=1,
            grid=(max(o[2] // min(64, o[2]) for o in order),),
            in_specs=[spec(*o) for o in order],
            out_specs=pl.BlockSpec(memory_space=pl.ANY),
            scratch_shapes=[pltpu.SemaphoreType.DMA((len(parts),))],
        ),
        out_shape=jax.ShapeDtypeStruct((places * total, width), bf16),
        compiler_params=pltpu.CompilerParams(vmem_limit_bytes=40 << 20),
        cost_estimate=pl.CostEstimate(
            flops=0, bytes_accessed=4 * places * total * width, transcendentals=0
        ),
    )(place, *parts)


def merge_kernel(steps, block, total, pieces, base, place_ref, *refs):
    whole, held, sems = refs[-3], refs[-2], refs[-1]
    step = pl.program_id(0)
    slot = lax.rem(step, 2)

    def copy(at, side, m):
        rows = pl.ds(pl.multiple_of(base + at * block, block), block)
        return pltpu.make_async_copy(
            held.at[side, m], whole.at[rows, place_ref[0] ^ m, :], sems.at[side, m]
        )

    def widen(m, which):
        value = refs[2 * m * pieces + which][...].astype(f32)
        for p in range(1, pieces):
            value = value + refs[2 * (m * pieces + p) + which][...].astype(f32)
        held[slot, m] = value

    for m in range(total):

        @pl.when(step >= 2)
        def _():
            copy(step - 2, slot, m).wait()

        @pl.when(step < steps // 2)
        def _():
            widen(m, 0)

        @pl.when(step >= steps // 2)
        def _():
            widen(m, 1)

        copy(step, slot, m).start()

    @pl.when(step == steps - 1)
    def _():
        for m in range(total):
            copy(step - 1, 1 - slot, m).wait()
            copy(step, slot, m).wait()


def merge_parts(place, parts, total, base, rows_total, whole=None):
    rows, width = parts[0].shape
    pieces = len(parts) // (2 * total)
    block = min(64, rows)
    steps = 2 * rows // block
    more = [] if whole is None else [whole]
    upper = pl.BlockSpec((block, width), lambda i, s: (jnp.minimum(i, steps // 2 - 1), 0))
    lower = pl.BlockSpec((block, width), lambda i, s: (jnp.maximum(i - steps // 2, 0), 0))
    return pl.pallas_call(
        functools.partial(merge_kernel, steps, block, total, pieces, base),
        grid_spec=pltpu.PrefetchScalarGridSpec(
            num_scalar_prefetch=1,
            grid=(steps,),
            in_specs=[upper, lower] * (len(parts) // 2)
            + [pl.BlockSpec(memory_space=pl.ANY)] * len(more),
            out_specs=pl.BlockSpec(memory_space=pl.ANY),
            scratch_shapes=[
                pltpu.VMEM((2, total, block, width), f32),
                pltpu.SemaphoreType.DMA((2, total)),
            ],
        ),
        out_shape=jax.ShapeDtypeStruct((rows_total, total, width), f32),
        input_output_aliases={1 + len(parts): 0} if more else {},
        compiler_params=pltpu.CompilerParams(vmem_limit_bytes=36 << 20),
        cost_estimate=pl.CostEstimate(
            flops=0,
            bytes_accessed=2 * len(parts) * rows * width + 8 * total * rows * width,
            transcendentals=0,
        ),
    )(place, *parts, *more)


def gather_rows(values, total):
    return jnp.concatenate(
        [values] + [from_peer(values, j, total) for j in range(1, total)], 0
    )


def scatter_rows(partial, total):
    rows = partial.shape[0] // total
    result = partial[:rows]
    for j in range(1, total):
        piece = partial[j * rows : (j + 1) * rows].astype(bf16)
        result = result + from_peer(piece, j, total).astype(f32)
    return result


def spread_rows(values, total):
    return [values] + [from_peer(values, j, total) for j in range(1, total)]


def add_rows(refs):
    total = len(refs)
    result = refs[0][...]
    rows = result.shape[1] // total
    for j in range(1, total):
        other = refs[j][...]
        blocks = [other[:, (i ^ j) * rows : ((i ^ j) + 1) * rows] for i in range(total)]
        result = result + jnp.concatenate(blocks, 1)
    return result


def diagonal(size):
    first = lax.broadcasted_iota(jnp.int32, (size, size), 0)
    return first == lax.broadcasted_iota(jnp.int32, (size, size), 1)


def as_column(row):
    return jnp.sum(jnp.where(diagonal(row.shape[1]), row, 0.0), 1, keepdims=True)


def as_row(column):
    return jnp.sum(jnp.where(diagonal(column.shape[0]), column, 0.0), 0, keepdims=True)


def dot_nn(a, b):
    return lax.dot_general(a, b, (((1,), (0,)), ((), ())), preferred_element_type=f32)


def expert_kernel(
    steps,
    mine_ref,
    rows_ref,
    cots_ref,
    router_ref,
    gate_w,
    up_w,
    down_w,
    back_ref,
    out_ref,
    grads_ref,
    ggate_ref,
    gup_ref,
    hidden_ref,
    total_out,
    total_back,
    weight,
):
    step = pl.program_id(0)
    mine = mine_ref[0]
    width = rows_ref.shape[1]
    expert_total = router_ref.shape[1]

    @pl.when(step == 0)
    def _():
        logits = dot_nn(rows_ref[...], router_ref[...])
        logits = jnp.exp(logits - jnp.max(logits, -1, keepdims=True))
        column = lax.broadcasted_iota(jnp.int32, logits.shape, 1)
        chosen = jnp.sum(jnp.where(column == mine, logits, 0.0), -1, keepdims=True)
        weight[...] = chosen / jnp.sum(logits, -1, keepdims=True)
        grads_ref[...] = (weight[...] * cots_ref[...].astype(f32)).astype(bf16)
        total_out[...] = jnp.zeros_like(total_out)
        total_back[...] = jnp.zeros_like(total_back)

    gate = dot_nn(rows_ref[...], gate_w[...])
    up = dot_nn(rows_ref[...], up_w[...])
    grad_hidden = dot_nn(grads_ref[...], down_w[...])
    sigma = jax.nn.sigmoid(gate)
    swish = gate * sigma
    hidden = (swish * up).astype(bf16)
    grad_gate = (grad_hidden * up * sigma * (1.0 + gate * (1.0 - sigma))).astype(bf16)
    grad_up = (grad_hidden * swish).astype(bf16)
    hidden_ref[...] = hidden
    ggate_ref[...] = grad_gate
    gup_ref[...] = grad_up
    total_out[...] += mm_nt(hidden, down_w[...])
    total_back[...] += mm_nt(grad_gate, gate_w[...]) + mm_nt(grad_up, up_w[...])

    @pl.when(step == steps - 1)
    def _():
        result = total_out[...].astype(bf16).astype(f32)
        out_ref[...] = (weight[...] * result).astype(bf16)
        grad_weight = jnp.sum(cots_ref[...].astype(f32) * result, -1, keepdims=True)
        high = grad_weight.astype(bf16).astype(f32)
        low = grad_weight - high
        back_ref[:, :width] = total_back[...].astype(bf16)
        extra = back_ref.shape[1] - width
        column = lax.broadcasted_iota(jnp.int32, (rows_ref.shape[0], extra), 1)
        side = jnp.where(column == mine, high, 0.0) + jnp.where(
            column == expert_total + mine, low, 0.0
        )
        back_ref[:, width:] = side.astype(bf16)


def run_expert(mine, rows, cots, router, expert, extra):
    count, width = rows.shape
    ff = expert.shape[1] // 3
    block = min(256, ff)
    steps = ff // block
    whole = pl.BlockSpec((count, width), lambda i, s: (0, 0))
    part = pl.BlockSpec((count, block), lambda i, s: (0, i))
    return pl.pallas_call(
        functools.partial(expert_kernel, steps),
        grid_spec=pltpu.PrefetchScalarGridSpec(
            num_scalar_prefetch=1,
            grid=(steps,),
            in_specs=[
                whole,
                whole,
                pl.BlockSpec(router.shape, lambda i, s: (0, 0)),
                pl.BlockSpec((width, block), lambda i, s: (0, i)),
                pl.BlockSpec((width, block), lambda i, s: (0, steps + i)),
                pl.BlockSpec((width, block), lambda i, s: (0, 2 * steps + i)),
            ],
            out_specs=[
                pl.BlockSpec((count, width + extra), lambda i, s: (0, 0)),
                whole,
                whole,
                part,
                part,
                part,
            ],
            scratch_shapes=[
                pltpu.VMEM((count, width), f32),
                pltpu.VMEM((count, width), f32),
                pltpu.VMEM((count, 1), f32),
            ],
        ),
        out_shape=[
            jax.ShapeDtypeStruct((count, width + extra), bf16),
            jax.ShapeDtypeStruct((count, width), bf16),
            jax.ShapeDtypeStruct((count, width), bf16),
            jax.ShapeDtypeStruct((count, ff), bf16),
            jax.ShapeDtypeStruct((count, ff), bf16),
            jax.ShapeDtypeStruct((count, ff), bf16),
        ],
        compiler_params=pltpu.CompilerParams(vmem_limit_bytes=48 << 20),
        cost_estimate=pl.CostEstimate(
            flops=12 * count * width * ff,
            bytes_accessed=6 * width * ff + 10 * count * width,
            transcendentals=count * ff,
        ),
    )(mine, rows, cots, router, expert, expert, expert)


def weight_kernel(groups, steps, place_ref, *refs):
    step = pl.program_id(0)
    outs = refs[5 * groups : 5 * groups + 4]
    left, right = refs[-2], refs[-1]
    count = refs[0].shape[0]

    def gather(into, which):
        for g in range(groups):
            into[g * count : (g + 1) * count, :] = refs[5 * g + which][...]

    @pl.when(step == 0)
    def _():
        gather(left, 0)

    @pl.when(step == 2 * steps)
    def _():
        gather(left, 1)

    @pl.when(step < steps)
    def _():
        gather(right, 2)

    @pl.when((step >= steps) & (step < 2 * steps))
    def _():
        gather(right, 3)

    @pl.when(step >= 2 * steps)
    def _():
        gather(right, 4)

    result = mm_tn(left[...], right[...]).astype(bf16)
    rows = outs[0].shape[0]
    for n, out_ref in enumerate(outs):
        out_ref[...] = result[n * rows : (n + 1) * rows]


def weight_grad(place, groups, columns):
    count, _ = groups[0][0].shape
    ff = groups[0][2].shape[1]
    block = min(512, ff)
    steps = ff // block
    side = pl.BlockSpec((count, columns), lambda i, s: (0, s[0]))

    def part(first):
        return pl.BlockSpec(
            (count, block),
            lambda i, s: (0, jnp.clip(i - first * steps, 0, steps - 1)),
        )

    return pl.pallas_call(
        functools.partial(weight_kernel, len(groups), steps),
        grid_spec=pltpu.PrefetchScalarGridSpec(
            num_scalar_prefetch=1,
            grid=(3 * steps,),
            in_specs=[side, side, part(0), part(1), part(2)] * len(groups),
            out_specs=[pl.BlockSpec((columns // 4, block), lambda i, s: (0, i))] * 4,
            scratch_shapes=[
                pltpu.VMEM((len(groups) * count, columns), bf16),
                pltpu.VMEM((len(groups) * count, block), bf16),
            ],
        ),
        out_shape=[jax.ShapeDtypeStruct((columns // 4, 3 * ff), bf16)] * 4,
        compiler_params=pltpu.CompilerParams(vmem_limit_bytes=48 << 20),
        cost_estimate=pl.CostEstimate(
            flops=6 * len(groups) * count * columns * ff,
            bytes_accessed=6 * columns * ff + 10 * len(groups) * count * ff,
            transcendentals=0,
        ),
    )(place, *[a for group in groups for a in group])


def collect_kernel(total, *refs):
    places, parts, out_ref, rows = refs[0], refs[1 : 1 + total], refs[-2], refs[-1]
    count = parts[0].shape[0]
    for j in range(total):
        rows[j * count : (j + 1) * count, :] = parts[j][...]
    out_ref[...] = dot_nn(places[...], rows[...]).astype(bf16)


def collect_rows(places, parts):
    tokens, count = places.shape
    rows, width = parts[0].shape
    block = 512 if width % 512 == 0 else 768
    return pl.pallas_call(
        functools.partial(collect_kernel, len(parts)),
        grid=(pl.cdiv(width, block),),
        in_specs=[pl.BlockSpec((tokens, count), lambda i: (0, 0))]
        + [pl.BlockSpec((rows, block), lambda i: (0, i))] * len(parts),
        out_specs=pl.BlockSpec((tokens, block), lambda i: (0, i)),
        out_shape=jax.ShapeDtypeStruct((tokens, width), bf16),
        scratch_shapes=[pltpu.VMEM((count, block), bf16)],
        compiler_params=pltpu.CompilerParams(vmem_limit_bytes=48 << 20),
        cost_estimate=pl.CostEstimate(
            flops=2 * tokens * count * width,
            bytes_accessed=2 * count * (width + tokens) + 2 * tokens * width,
            transcendentals=0,
        ),
    )(places, *parts)


def turn(values, cosine, sine):
    return values * cosine + pltpu.roll(values, HD // 2, 1) * sine


def head_forward(raw_q, raw_k, scale, gains, cosine, sine, row_pos, col_pos):
    query = turn(raw_q * scale[:, 0:1] * gains[0:1, :], cosine, sine).astype(bf16)
    key = turn(raw_k * scale[:, 1:2] * gains[1:2, :], cosine, sine).astype(bf16)
    scores = mm_nt(query, key) * (1.0 / math.sqrt(HD))
    scores = jnp.where(col_pos <= row_pos, scores, neg_large)
    weights = jnp.exp(scores - jnp.max(scores, -1, keepdims=True))
    return query, key, weights / jnp.sum(weights, -1, keepdims=True)


def attend_kernel(model_width, q_ref, k_ref, v_ref, gain_ref, cos_ref, sin_ref, rp, cp, *refs):
    parts, out_ref, scale_ref = refs[:-2], refs[-2], refs[-1]

    @pl.when(pl.program_id(0) == 0)
    def _():
        scale = lax.rsqrt(add_rows(parts) / model_width + epsilon)
        for n in range(2):
            scale_ref[:, n : n + 1] = as_column(scale[n : n + 1, :])

    _, _, probs = head_forward(
        q_ref[...],
        k_ref[...],
        scale_ref[...],
        gain_ref[...],
        cos_ref[...],
        sin_ref[...],
        rp[...],
        cp[...],
    )
    out_ref[...] = dot_nn(probs.astype(bf16), v_ref[...].astype(bf16)).astype(bf16)


def attend_back_kernel(
    q_ref,
    k_ref,
    v_ref,
    gain_ref,
    cos_ref,
    sin_ref,
    rp,
    cp,
    scale_ref,
    grad_ref,
    yq_ref,
    yk_ref,
    gv_ref,
    dots_ref,
    gains_ref,
    held,
):
    head = pl.program_id(0)
    raw_q = q_ref[...]
    raw_k = k_ref[...]
    scale = scale_ref[...]
    gains = gain_ref[...]
    query, key, probs = head_forward(
        raw_q, raw_k, scale, gains, cos_ref[...], sin_ref[...], rp[...], cp[...]
    )
    grad = grad_ref[...]
    grad_prob = mm_nt(grad, v_ref[...].astype(bf16))
    delta = jnp.sum(probs * grad_prob, -1, keepdims=True)
    grad_scores = (probs * (grad_prob - delta)).astype(bf16)
    gv_ref[...] = mm_tn(probs.astype(bf16), grad).astype(bf16)
    soft = 1.0 / math.sqrt(HD)
    back_sine = -sin_ref[...]
    grad_q = turn(dot_nn(grad_scores, key) * soft, cos_ref[...], back_sine)
    grad_k = turn(mm_tn(grad_scores, query) * soft, cos_ref[...], back_sine)
    yq_ref[...] = grad_q
    yk_ref[...] = grad_k
    part_q = grad_q * raw_q
    part_k = grad_k * raw_k
    gains_ref[0:1, :] = jnp.sum(part_q * scale[:, 0:1], 0, keepdims=True)
    gains_ref[1:2, :] = jnp.sum(part_k * scale[:, 1:2], 0, keepdims=True)
    dot_q = jnp.sum(part_q * gains[0:1, :], -1, keepdims=True)
    dot_k = jnp.sum(part_k * gains[1:2, :], -1, keepdims=True)

    @pl.when(head == 0)
    def _():
        held[...] = jnp.zeros_like(held)

    held[:, 0:1] += dot_q
    held[:, 1:2] += dot_k

    @pl.when(head == pl.num_programs(0) - 1)
    def _():
        for n in range(2):
            dots_ref[n : n + 1, :] = as_row(held[:, n : n + 1])


def finish_kernel(model_width, heads, yq_ref, yk_ref, gv_ref, raw_ref, gain_ref, scale_ref, *refs):
    parts, out_ref, dots = refs[:-2], refs[-2], refs[-1]
    step = pl.program_id(0)

    @pl.when(step == 0)
    def _():
        total = add_rows(parts) / model_width
        for n in range(2):
            dots[:, n : n + 1] = as_column(total[n : n + 1, :])

    def through(n, grad):
        scale = scale_ref[:, n : n + 1]
        cube = scale * scale * scale * dots[:, n : n + 1]
        out_ref[...] = (scale * (grad * gain_ref[n : n + 1, :]) - raw_ref[...] * cube).astype(bf16)

    @pl.when(step < heads)
    def _():
        through(0, yq_ref[...])

    @pl.when((step >= heads) & (step < 2 * heads))
    def _():
        through(1, yk_ref[...])

    @pl.when(step >= 2 * heads)
    def _():
        out_ref[...] = gv_ref[...]


def finish(model_width, yq, yk, gv, raw_qkv, gains, scales, parts):
    seq, width = gv.shape
    heads = width // HD

    def block(first, last):
        return pl.BlockSpec((seq, HD), lambda i: (0, jnp.clip(i - first, 0, last)))

    return pl.pallas_call(
        functools.partial(finish_kernel, model_width, heads),
        grid=(3 * heads,),
        in_specs=[
            block(0, heads - 1),
            block(heads, heads - 1),
            block(2 * heads, heads - 1),
            block(0, 2 * heads - 1),
            pl.BlockSpec((2, HD), lambda i: (0, lax.rem(i, heads))),
            pl.BlockSpec((seq, 2), lambda i: (0, 0)),
        ]
        + [pl.BlockSpec((2, seq), lambda i: (0, 0))] * len(parts),
        out_specs=pl.BlockSpec((seq, HD), lambda i: (0, i)),
        out_shape=jax.ShapeDtypeStruct((seq, 3 * width), bf16),
        scratch_shapes=[pltpu.VMEM((seq, 2), f32)],
        compiler_params=pltpu.CompilerParams(vmem_limit_bytes=48 << 20),
        cost_estimate=pl.CostEstimate(
            flops=16 * seq * width, bytes_accessed=26 * seq * width, transcendentals=0
        ),
    )(yq, yk, gv, raw_qkv, gains, scales, *parts)


def head_specs(seq, heads):
    one = pl.BlockSpec((seq, HD), lambda h: (0, h))
    key = pl.BlockSpec((seq, HD), lambda h: (0, heads + h))
    value = pl.BlockSpec((seq, HD), lambda h: (0, 2 * heads + h))

    def fixed(shape):
        return pl.BlockSpec(shape, lambda h: (0, 0))

    specs = [
        one,
        key,
        value,
        pl.BlockSpec((2, HD), lambda h: (0, h)),
        fixed((seq, HD)),
        fixed((seq, HD)),
        fixed((seq, 1)),
        fixed((1, seq)),
    ]
    return one, specs, fixed


def attend(raw_qkv, tables, parts, model_width):
    seq = raw_qkv.shape[0]
    width = raw_qkv.shape[1] // 3
    heads = width // HD
    one, specs, fixed = head_specs(seq, heads)
    return pl.pallas_call(
        functools.partial(attend_kernel, model_width),
        grid=(heads,),
        in_specs=specs + [fixed((2, seq))] * len(parts),
        out_specs=[one, fixed((seq, 2))],
        out_shape=[
            jax.ShapeDtypeStruct((seq, width), bf16),
            jax.ShapeDtypeStruct((seq, 2), f32),
        ],
        compiler_params=pltpu.CompilerParams(vmem_limit_bytes=48 << 20),
        cost_estimate=pl.CostEstimate(
            flops=4 * seq * seq * width,
            bytes_accessed=12 * seq * width,
            transcendentals=seq * seq * heads,
        ),
    )(raw_qkv, raw_qkv, raw_qkv, *tables, *parts)


def attend_back(raw_qkv, tables, scales, grad):
    seq, width = grad.shape
    heads = width // HD
    one, specs, fixed = head_specs(seq, heads)
    return pl.pallas_call(
        attend_back_kernel,
        grid=(heads,),
        in_specs=specs + [fixed((seq, 2)), one],
        out_specs=[one, one, one, fixed((2, seq)), pl.BlockSpec((2, HD), lambda h: (0, h))],
        out_shape=[
            jax.ShapeDtypeStruct((seq, width), f32),
            jax.ShapeDtypeStruct((seq, width), f32),
            jax.ShapeDtypeStruct((seq, width), bf16),
            jax.ShapeDtypeStruct((2, seq), f32),
            jax.ShapeDtypeStruct((2, width), f32),
        ],
        scratch_shapes=[pltpu.VMEM((seq, 2), f32)],
        compiler_params=pltpu.CompilerParams(vmem_limit_bytes=56 << 20),
        cost_estimate=pl.CostEstimate(
            flops=12 * seq * seq * width,
            bytes_accessed=24 * seq * width,
            transcendentals=seq * seq * heads,
        ),
    )(raw_qkv, raw_qkv, raw_qkv, *tables, scales, grad)


def layer(
    tokens,
    attn_gain,
    query_gain,
    key_gain,
    w_query,
    w_key,
    w_value,
    output_weight,
    ffn_gain,
    router,
    experts,
    routes,
    cotangent,
):
    row_total = tokens.shape[1]
    half_rows = row_total // 2
    model_width = tokens.shape[2]
    expert_total = router.shape[1]
    slice_rows = experts.shape[0]
    local_experts = experts.shape[1]
    top_count = routes.shape[2]
    ff = experts.shape[2] // 3
    C = lax.axis_size(CTX)
    F = lax.axis_size(FSDP)
    devices = C * F
    W = model_width // C
    seq = C * row_total
    shard = w_query.shape[0]
    pieces = C // local_experts
    cap_unit = 16 * expert_total * pieces
    piece_cap = (17 * row_total * top_count + cap_unit - 1) // cap_unit
    me = lax.axis_index(CTX)
    row = lax.axis_index(FSDP)
    my_expert = row * local_experts + me // pieces
    my_column = me * W

    tokens_low = tokens.reshape(row_total, model_width)
    tokens_seq = gather_rows(tokens_low, C)
    route_ids = routes.reshape(row_total, top_count)
    column_ids = lax.all_gather(route_ids, FSDP, axis=0, tiled=True)

    def by_column(weight):
        return jnp.swapaxes(weight.reshape(shard, C, W), 0, 1)

    w_cols = lax.all_to_all(
        jnp.concatenate([by_column(w_query), by_column(w_key), by_column(w_value)], 2),
        CTX,
        split_axis=0,
        concat_axis=0,
        tiled=True,
    )
    w_qkv = lax.all_gather(w_cols, FSDP, axis=1, tiled=True).reshape(model_width, 3 * W)
    w_o = lax.all_gather(output_weight, FSDP, axis=0, tiled=True)

    by_expert = lax.optimization_barrier(
        jnp.swapaxes(lax.optimization_barrier(experts), 0, 1)
    )
    half = slice_rows // 2

    def expert_slice(array, j, begin, rows):
        first = ((me ^ j) // pieces, begin, 0)
        return lax.dynamic_slice(array, first, (1, rows, 3 * ff)).reshape(rows, 3 * ff)

    near = [j for j in range(1, C) if j & (j - 1) == 0]
    far = [j for j in range(1, C) if j not in near]
    eighth = slice_rows // 8
    near_cuts = [(j, part * half, half) for part in range(2) for j in near]
    far_cuts = [(j, part * eighth, eighth) for part in range(8) for j in far]
    cut = [expert_slice(by_expert, *o) for o in near_cuts]
    cut, later_expert = lax.optimization_barrier((cut, by_expert))
    own = [later_expert] * 2
    order = [(0, 0, half), (0, half, half)]
    for o, piece in zip(near_cuts, cut):
        order.append(o)
        own.append(from_peer(piece, o[0], C))
    for o in far_cuts:
        order.append(o)
        piece = expert_slice(later_expert, *o)
        own.append(from_peer(piece, o[0], C))
    expert = place_parts(me.reshape(1), pieces, tuple(order), own, slice_rows)

    column_rows = F * row_total
    member = jnp.sum(
        (column_ids[:, :, None] == jnp.arange(expert_total, dtype=jnp.int32)).astype(f32), 1
    )
    order = jnp.arange(row_total, dtype=jnp.int32)
    earlier = jnp.einsum(
        "ts,fse->fte",
        (order[None, :] < order[:, None]).astype(bf16),
        member.astype(bf16).reshape(F, row_total, expert_total),
        preferred_element_type=f32,
    ).reshape(column_rows, expert_total)
    marked = jnp.where(member > 0.5, earlier, -1.0).T
    group_rows = F * piece_cap
    group_ids = jnp.arange(group_rows, dtype=jnp.int32)
    token_block = jnp.arange(column_rows, dtype=jnp.int32) // row_total
    same_block = (group_ids // piece_cap)[:, None] == token_block[None, :]
    selects = []
    places = []
    for j in range(C):
        target = me ^ j
        mark = lax.dynamic_slice_in_dim(marked, row * local_experts + target // pieces, 1, 0)
        slot = (target % pieces) * piece_cap + group_ids % piece_cap
        slot = slot.astype(f32)
        selects.append(((mark == slot[:, None]) & same_block).astype(bf16))
        places.append(((mark.T == slot[None, :]) & same_block.T).astype(bf16))

    def exchange(parts):
        result = []
        for j in range(C):
            if j == 0:
                result.append(parts[j])
            else:
                result.append(from_peer(parts[j], j, C))
        return result

    def deliver(values):
        parts = [mm(select, values).astype(bf16) for select in selects]
        return exchange(parts)

    def collect(parts):
        return collect_rows(places, parts)

    cot_low = cotangent.reshape(row_total, model_width)
    cot_column = lax.all_gather(cot_low, FSDP, axis=0, tiled=True)
    cot_rows = deliver(cot_column)

    place = me ^ jnp.arange(C, dtype=jnp.int32)
    within = jnp.arange(half_rows, dtype=jnp.int32)
    positions = jnp.concatenate(
        [
            place[:, None] * half_rows + within,
            (2 * C - 1 - place)[:, None] * half_rows + within,
        ],
        1,
    ).reshape(seq)
    cosine, sine = rope_tables(positions, HD)
    inputs_seq = tokens_seq.astype(f32)
    scale_one = inv_rms(inputs_seq)
    normed = (inputs_seq * scale_one * attn_gain).astype(bf16)
    gains = lax.dynamic_slice_in_dim(jnp.stack([query_gain, key_gain]), my_column, W, 1)
    places = jnp.concatenate(places, 1)
    w_qkv, selects, places = lax.optimization_barrier((w_qkv, selects, places))
    raw_qkv = mm(normed, w_qkv)
    raw_q = raw_qkv[:, :W]
    raw_k = raw_qkv[:, W : 2 * W]
    squares = spread_rows(jnp.stack([jnp.sum(raw_q * raw_q, -1), jnp.sum(raw_k * raw_k, -1)]), C)
    signed_sine = jnp.where(jnp.arange(HD) < HD // 2, -1.0, 1.0) * sine
    tables = (gains, cosine, signed_sine, positions.reshape(seq, 1), positions.reshape(1, seq))
    attended, scales = attend(raw_qkv, tables, squares, model_width)
    inputs = tokens_low.astype(f32)
    hidden_one = inputs + scatter_rows(mm(attended, w_o), C)

    scale_two = inv_rms(hidden_one)
    ffn_in = (hidden_one * scale_two * ffn_gain).astype(bf16)
    probs = jax.nn.softmax(mm(ffn_in, router), -1)
    ffn_column = lax.all_gather(ffn_in, FSDP, axis=0, tiled=True)
    expert_in = deliver(ffn_column)
    extra = -(-2 * expert_total // 128) * 128
    done = []
    mine = my_expert.reshape(1)
    for j in range(C):
        result = run_expert(mine, expert_in[j], cot_rows[j], router, expert, extra)
        if j == 0:
            result, mine = lax.optimization_barrier((result, mine))
        done.append(result)
    back = collect(exchange([d[0] for d in done]))
    back = lax.psum_scatter(back, FSDP, scatter_dimension=0, tiled=True).astype(f32)
    groups = [(expert_in[j], done[j][2], done[j][3], done[j][4], done[j][5]) for j in range(C)]
    d_own = []
    for j in range(C):
        d_own.append(weight_grad((me ^ j).reshape(1), groups, slice_rows))
    arrived = {}
    for j in range(C):
        for part in range(4):
            if j == 0:
                arrived[j, part] = d_own[j][part]
            else:
                arrived[j, part] = from_peer(d_own[j][part], j, C)
    d_experts = None
    for part in range(2):
        d_experts = merge_parts(
            (me // pieces).reshape(1),
            [arrived[j, 2 * part + n] for j in range(C) for n in range(2)],
            local_experts,
            part * half,
            slice_rows,
            d_experts,
        )
    mixed = collect(exchange([d[1] for d in done]))
    mixed = lax.psum_scatter(mixed, FSDP, scatter_dimension=0, tiled=True).astype(f32)

    grad_probs = (
        back[:, model_width : model_width + expert_total]
        + back[:, model_width + expert_total : model_width + 2 * expert_total]
    )
    grad_logits = (probs * (grad_probs - jnp.sum(probs * grad_probs, -1, keepdims=True))).astype(
        bf16
    )
    grad_ffn = back[:, :model_width] + mm_nt(grad_logits, router)
    grad_router = mm_tn(grad_logits, ffn_in)
    grad_hidden_one, grad_ffn_gain = norm_back(grad_ffn, hidden_one, scale_two, ffn_gain)
    grad_hidden_one = grad_hidden_one + cot_low.astype(f32)
    share = model_width // devices
    sums = jnp.concatenate(
        [grad_router.reshape(devices, -1), grad_ffn_gain.reshape(devices, share)], 1
    )
    sums = jnp.sum(lax.all_to_all(sums[:, None], everyone, 0, 0, tiled=True), 0)
    sums = lax.all_to_all(
        jnp.broadcast_to(sums, (devices,) + sums.shape), everyone, 0, 0, tiled=True
    ).reshape(devices, -1)
    d_ffn_gain = sums[:, -share:].reshape(model_width)
    d_router = sums[:, :-share].reshape(expert_total, model_width).T

    branch_seq = gather_rows(grad_hidden_one.astype(bf16), C)
    grad_att = mm_nt(branch_seq, w_o).astype(bf16)
    d_output = mm_tn(attended, branch_seq).astype(bf16)
    grad_att, d_output = lax.optimization_barrier((grad_att, d_output))

    d_output = lax.psum_scatter(d_output, FSDP, scatter_dimension=0, tiled=True).astype(f32)
    grad_q_n, grad_k_n, grad_value, dots, gain_grads = attend_back(
        raw_qkv, tables, scales, grad_att
    )
    dots = spread_rows(dots, C)
    late_hidden, dots = lax.optimization_barrier((hidden_one, dots))
    output = (late_hidden + mixed).astype(bf16).reshape(1, row_total, model_width)
    grad_qkv = finish(
        model_width, grad_q_n, grad_k_n, grad_value, raw_qkv, gains, scales, dots
    )
    d_cols = lax.psum_scatter(
        mm_tn(normed, grad_qkv).astype(bf16).reshape(C, F * shard, 3 * W),
        FSDP,
        scatter_dimension=1,
        tiled=True,
    )
    received = []
    for j in range(C):
        piece = lax.dynamic_index_in_dim(d_cols, me ^ j, 0, keepdims=False)
        received.append(from_peer(piece, j, C) if j else piece)
    received = jnp.stack(received)
    received = [
        lax.dynamic_index_in_dim(received, me ^ c, 0, keepdims=False) for c in range(C)
    ]
    d_qkv = [
        jnp.concatenate([r[:, n * W : (n + 1) * W] for r in received], 1).astype(f32)
        for n in range(3)
    ]

    grad_normed = scatter_rows(mm_nt(grad_qkv, w_qkv), C)
    grad_inputs, grad_attn_gain = norm_back(grad_normed, inputs, scale_one[:row_total], attn_gain)
    grad_inputs = grad_inputs + grad_hidden_one

    vector = jnp.concatenate([grad_attn_gain, gain_grads[0], gain_grads[1]]).reshape(1, -1, 128)
    everything = lax.all_to_all(
        jnp.broadcast_to(vector, (devices,) + vector.shape[1:]), everyone, 0, 0, tiled=True
    ).reshape(devices, -1)
    d_attn_gain = jnp.sum(everything[:, :model_width], 0)
    by_place = jnp.sum(everything[:, model_width:].reshape(F, C, 2, W), 0)
    d_query_gain = by_place[:, 0].reshape(model_width)
    d_key_gain = by_place[:, 1].reshape(model_width)

    return (
        output,
        grad_inputs.reshape(1, row_total, model_width),
        d_attn_gain,
        d_query_gain,
        d_key_gain,
        d_qkv[0],
        d_qkv[1],
        d_qkv[2],
        d_output,
        d_ffn_gain,
        d_router,
        d_experts,
    )


def solution(mesh):
    placed = (
        P(FSDP, CTX, None),
        P(),
        P(),
        P(),
        P((CTX, FSDP), None),
        P((CTX, FSDP), None),
        P((CTX, FSDP), None),
        P((CTX, FSDP), None),
        P(),
        P(),
        P(CTX, FSDP, None),
        P(FSDP, CTX, None),
        P(FSDP, CTX, None),
    )
    return jax.shard_map(
        layer,
        mesh=mesh,
        in_specs=placed,
        out_specs=(
            P(FSDP, CTX, None),
            P(FSDP, CTX, None),
            P(),
            P(),
            P(),
            P((CTX, FSDP), None),
            P((CTX, FSDP), None),
            P((CTX, FSDP), None),
            P((CTX, FSDP), None),
            P(),
            P(),
            P(CTX, FSDP, None),
        ),
        check_vma=False,
    )
```

```python
import functools
import math

import jax
import jax.numpy as jnp
from jax import lax
from jax.experimental import pallas as pl
from jax.experimental.pallas import tpu as pltpu
from jax.sharding import PartitionSpec as P

HD = 128

epsilon = 1e-05
neg_large = -1e30
f32 = jnp.float32
bf16 = jnp.bfloat16
CTX = "ctx"
FSDP = "fsdp"
everyone = (FSDP, CTX)


def mm(a, b):
    return jnp.dot(a, b, preferred_element_type=f32)


def mm_nt(a, b):
    return lax.dot_general(a, b, (((1,), (1,)), ((), ())), preferred_element_type=f32)


def mm_tn(a, b):
    return lax.dot_general(a, b, (((0,), (0,)), ((), ())), preferred_element_type=f32)


def inv_rms(values):
    return lax.rsqrt(jnp.mean(values * values, -1, keepdims=True) + epsilon)


def norm_back(grad, values, scale, gain):
    weighted = grad * gain
    grad_values = scale * weighted - values * scale * scale * scale * jnp.mean(
        weighted * values, -1, keepdims=True
    )
    grad_gain = jnp.sum(grad * values * scale, axis=0)
    return (grad_values, grad_gain)


def rope_tables(positions, head_size):
    half_size = head_size // 2
    inverse_freq = jnp.exp(
        jnp.arange(half_size, dtype=f32) * (-2.0 * math.log(10000.0) / head_size)
    )
    angles = positions.astype(f32)[:, None] * inverse_freq[None, :]
    cosine = jnp.cos(angles)
    sine = jnp.sin(angles)
    return (jnp.concatenate([cosine, cosine], -1), jnp.concatenate([sine, sine], -1))


def from_peer(values, offset, total):
    return lax.ppermute(values, CTX, [(i, i ^ offset) for i in range(total)])


def place_kernel(order, total, place_ref, *refs):
    parts, whole, sems = refs[:-2], refs[-2], refs[-1]
    step = pl.program_id(0)

    def copy(n):
        j, begin, rows = order[n]
        block = min(64, rows)
        first = pl.multiple_of((place_ref[0] ^ j) * total + begin + step * block, block)
        part = parts[n].at[0] if j == 0 else parts[n]
        return pltpu.make_async_copy(part, whole.at[pl.ds(first, block), :], sems.at[n])

    for n in range(len(parts)):

        @pl.when(step < order[n][2] // min(64, order[n][2]))
        def _():
            copy(n).start()

    for n in range(len(parts)):

        @pl.when(step < order[n][2] // min(64, order[n][2]))
        def _():
            copy(n).wait()


def place_parts(place, pieces, order, parts, total):
    width = parts[0].shape[-1]
    places = max(o[0] for o in order) + 1

    def spec(j, begin, rows):
        block = min(64, rows)
        last = rows // block - 1
        if j == 0:
            return pl.BlockSpec(
                (1, block, width),
                lambda i, s: (s[0] // pieces, begin // block + jnp.minimum(i, last), 0),
            )
        return pl.BlockSpec((block, width), lambda i, s: (jnp.minimum(i, last), 0))

    return pl.pallas_call(
        functools.partial(place_kernel, order, total),
        grid_spec=pltpu.PrefetchScalarGridSpec(
            num_scalar_prefetch=1,
            grid=(max(o[2] // min(64, o[2]) for o in order),),
            in_specs=[spec(*o) for o in order],
            out_specs=pl.BlockSpec(memory_space=pl.ANY),
            scratch_shapes=[pltpu.SemaphoreType.DMA((len(parts),))],
        ),
        out_shape=jax.ShapeDtypeStruct((places * total, width), bf16),
        compiler_params=pltpu.CompilerParams(vmem_limit_bytes=40 << 20),
        cost_estimate=pl.CostEstimate(
            flops=0, bytes_accessed=4 * places * total * width, transcendentals=0
        ),
    )(place, *parts)


def merge_kernel(steps, block, total, pieces, base, place_ref, *refs):
    whole, held, sems = refs[-3], refs[-2], refs[-1]
    step = pl.program_id(0)
    slot = lax.rem(step, 2)

    def copy(at, side, m):
        rows = pl.ds(pl.multiple_of(base + at * block, block), block)
        return pltpu.make_async_copy(
            held.at[side, m], whole.at[rows, place_ref[0] ^ m, :], sems.at[side, m]
        )

    def widen(m, which):
        value = refs[2 * m * pieces + which][...].astype(f32)
        for p in range(1, pieces):
            value = value + refs[2 * (m * pieces + p) + which][...].astype(f32)
        held[slot, m] = value

    for m in range(total):

        @pl.when(step >= 2)
        def _():
            copy(step - 2, slot, m).wait()

        @pl.when(step < steps // 2)
        def _():
            widen(m, 0)

        @pl.when(step >= steps // 2)
        def _():
            widen(m, 1)

        copy(step, slot, m).start()

    @pl.when(step == steps - 1)
    def _():
        for m in range(total):
            copy(step - 1, 1 - slot, m).wait()
            copy(step, slot, m).wait()


def merge_parts(place, parts, total, base, rows_total, whole=None):
    rows, width = parts[0].shape
    pieces = len(parts) // (2 * total)
    block = min(64, rows)
    steps = 2 * rows // block
    more = [] if whole is None else [whole]
    upper = pl.BlockSpec((block, width), lambda i, s: (jnp.minimum(i, steps // 2 - 1), 0))
    lower = pl.BlockSpec((block, width), lambda i, s: (jnp.maximum(i - steps // 2, 0), 0))
    return pl.pallas_call(
        functools.partial(merge_kernel, steps, block, total, pieces, base),
        grid_spec=pltpu.PrefetchScalarGridSpec(
            num_scalar_prefetch=1,
            grid=(steps,),
            in_specs=[upper, lower] * (len(parts) // 2)
            + [pl.BlockSpec(memory_space=pl.ANY)] * len(more),
            out_specs=pl.BlockSpec(memory_space=pl.ANY),
            scratch_shapes=[
                pltpu.VMEM((2, total, block, width), f32),
                pltpu.SemaphoreType.DMA((2, total)),
            ],
        ),
        out_shape=jax.ShapeDtypeStruct((rows_total, total, width), f32),
        input_output_aliases={1 + len(parts): 0} if more else {},
        compiler_params=pltpu.CompilerParams(vmem_limit_bytes=36 << 20),
        cost_estimate=pl.CostEstimate(
            flops=0,
            bytes_accessed=2 * len(parts) * rows * width + 8 * total * rows * width,
            transcendentals=0,
        ),
    )(place, *parts, *more)


def gather_rows(values, total):
    return jnp.concatenate(
        [values] + [from_peer(values, j, total) for j in range(1, total)], 0
    )


def scatter_rows(partial, total):
    rows = partial.shape[0] // total
    result = partial[:rows]
    for j in range(1, total):
        piece = partial[j * rows : (j + 1) * rows].astype(bf16)
        result = result + from_peer(piece, j, total).astype(f32)
    return result


def spread_rows(values, total):
    return [values] + [from_peer(values, j, total) for j in range(1, total)]


def add_rows(refs):
    total = len(refs)
    result = refs[0][...]
    rows = result.shape[1] // total
    for j in range(1, total):
        other = refs[j][...]
        blocks = [other[:, (i ^ j) * rows : ((i ^ j) + 1) * rows] for i in range(total)]
        result = result + jnp.concatenate(blocks, 1)
    return result


def diagonal(size):
    first = lax.broadcasted_iota(jnp.int32, (size, size), 0)
    return first == lax.broadcasted_iota(jnp.int32, (size, size), 1)


def as_column(row):
    return jnp.sum(jnp.where(diagonal(row.shape[1]), row, 0.0), 1, keepdims=True)


def as_row(column):
    return jnp.sum(jnp.where(diagonal(column.shape[0]), column, 0.0), 0, keepdims=True)


def dot_nn(a, b):
    return lax.dot_general(a, b, (((1,), (0,)), ((), ())), preferred_element_type=f32)


def expert_kernel(
    steps,
    mine_ref,
    rows_ref,
    cots_ref,
    router_ref,
    gate_w,
    up_w,
    down_w,
    back_ref,
    out_ref,
    grads_ref,
    ggate_ref,
    gup_ref,
    hidden_ref,
    total_out,
    total_back,
    weight,
):
    step = pl.program_id(0)
    mine = mine_ref[0]
    width = rows_ref.shape[1]
    expert_total = router_ref.shape[1]

    @pl.when(step == 0)
    def _():
        logits = dot_nn(rows_ref[...], router_ref[...])
        logits = jnp.exp(logits - jnp.max(logits, -1, keepdims=True))
        column = lax.broadcasted_iota(jnp.int32, logits.shape, 1)
        chosen = jnp.sum(jnp.where(column == mine, logits, 0.0), -1, keepdims=True)
        weight[...] = chosen / jnp.sum(logits, -1, keepdims=True)
        grads_ref[...] = (weight[...] * cots_ref[...].astype(f32)).astype(bf16)
        total_out[...] = jnp.zeros_like(total_out)
        total_back[...] = jnp.zeros_like(total_back)

    gate = dot_nn(rows_ref[...], gate_w[...])
    up = dot_nn(rows_ref[...], up_w[...])
    grad_hidden = dot_nn(grads_ref[...], down_w[...])
    sigma = jax.nn.sigmoid(gate)
    swish = gate * sigma
    hidden = (swish * up).astype(bf16)
    grad_gate = (grad_hidden * up * sigma * (1.0 + gate * (1.0 - sigma))).astype(bf16)
    grad_up = (grad_hidden * swish).astype(bf16)
    hidden_ref[...] = hidden
    ggate_ref[...] = grad_gate
    gup_ref[...] = grad_up
    total_out[...] += mm_nt(hidden, down_w[...])
    total_back[...] += mm_nt(grad_gate, gate_w[...]) + mm_nt(grad_up, up_w[...])

    @pl.when(step == steps - 1)
    def _():
        result = total_out[...].astype(bf16).astype(f32)
        out_ref[...] = (weight[...] * result).astype(bf16)
        grad_weight = jnp.sum(cots_ref[...].astype(f32) * result, -1, keepdims=True)
        high = grad_weight.astype(bf16).astype(f32)
        low = grad_weight - high
        back_ref[:, :width] = total_back[...].astype(bf16)
        extra = back_ref.shape[1] - width
        column = lax.broadcasted_iota(jnp.int32, (rows_ref.shape[0], extra), 1)
        side = jnp.where(column == mine, high, 0.0) + jnp.where(
            column == expert_total + mine, low, 0.0
        )
        back_ref[:, width:] = side.astype(bf16)


def run_expert(mine, rows, cots, router, expert, extra):
    count, width = rows.shape
    ff = expert.shape[1] // 3
    block = min(256, ff)
    steps = ff // block
    whole = pl.BlockSpec((count, width), lambda i, s: (0, 0))
    part = pl.BlockSpec((count, block), lambda i, s: (0, i))
    return pl.pallas_call(
        functools.partial(expert_kernel, steps),
        grid_spec=pltpu.PrefetchScalarGridSpec(
            num_scalar_prefetch=1,
            grid=(steps,),
            in_specs=[
                whole,
                whole,
                pl.BlockSpec(router.shape, lambda i, s: (0, 0)),
                pl.BlockSpec((width, block), lambda i, s: (0, i)),
                pl.BlockSpec((width, block), lambda i, s: (0, steps + i)),
                pl.BlockSpec((width, block), lambda i, s: (0, 2 * steps + i)),
            ],
            out_specs=[
                pl.BlockSpec((count, width + extra), lambda i, s: (0, 0)),
                whole,
                whole,
                part,
                part,
                part,
            ],
            scratch_shapes=[
                pltpu.VMEM((count, width), f32),
                pltpu.VMEM((count, width), f32),
                pltpu.VMEM((count, 1), f32),
            ],
        ),
        out_shape=[
            jax.ShapeDtypeStruct((count, width + extra), bf16),
            jax.ShapeDtypeStruct((count, width), bf16),
            jax.ShapeDtypeStruct((count, width), bf16),
            jax.ShapeDtypeStruct((count, ff), bf16),
            jax.ShapeDtypeStruct((count, ff), bf16),
            jax.ShapeDtypeStruct((count, ff), bf16),
        ],
        compiler_params=pltpu.CompilerParams(vmem_limit_bytes=48 << 20),
        cost_estimate=pl.CostEstimate(
            flops=12 * count * width * ff,
            bytes_accessed=6 * width * ff + 10 * count * width,
            transcendentals=count * ff,
        ),
    )(mine, rows, cots, router, expert, expert, expert)


def weight_kernel(groups, steps, place_ref, *refs):
    step = pl.program_id(0)
    outs = refs[5 * groups : 5 * groups + 4]
    left, right = refs[-2], refs[-1]
    count = refs[0].shape[0]

    def gather(into, which):
        for g in range(groups):
            into[g * count : (g + 1) * count, :] = refs[5 * g + which][...]

    @pl.when(step == 0)
    def _():
        gather(left, 0)

    @pl.when(step == 2 * steps)
    def _():
        gather(left, 1)

    @pl.when(step < steps)
    def _():
        gather(right, 2)

    @pl.when((step >= steps) & (step < 2 * steps))
    def _():
        gather(right, 3)

    @pl.when(step >= 2 * steps)
    def _():
        gather(right, 4)

    result = mm_tn(left[...], right[...]).astype(bf16)
    rows = outs[0].shape[0]
    for n, out_ref in enumerate(outs):
        out_ref[...] = result[n * rows : (n + 1) * rows]


def weight_grad(place, groups, columns):
    count, _ = groups[0][0].shape
    ff = groups[0][2].shape[1]
    block = min(512, ff)
    steps = ff // block
    side = pl.BlockSpec((count, columns), lambda i, s: (0, s[0]))

    def part(first):
        return pl.BlockSpec(
            (count, block),
            lambda i, s: (0, jnp.clip(i - first * steps, 0, steps - 1)),
        )

    return pl.pallas_call(
        functools.partial(weight_kernel, len(groups), steps),
        grid_spec=pltpu.PrefetchScalarGridSpec(
            num_scalar_prefetch=1,
            grid=(3 * steps,),
            in_specs=[side, side, part(0), part(1), part(2)] * len(groups),
            out_specs=[pl.BlockSpec((columns // 4, block), lambda i, s: (0, i))] * 4,
            scratch_shapes=[
                pltpu.VMEM((len(groups) * count, columns), bf16),
                pltpu.VMEM((len(groups) * count, block), bf16),
            ],
        ),
        out_shape=[jax.ShapeDtypeStruct((columns // 4, 3 * ff), bf16)] * 4,
        compiler_params=pltpu.CompilerParams(vmem_limit_bytes=48 << 20),
        cost_estimate=pl.CostEstimate(
            flops=6 * len(groups) * count * columns * ff,
            bytes_accessed=6 * columns * ff + 10 * len(groups) * count * ff,
            transcendentals=0,
        ),
    )(place, *[a for group in groups for a in group])


def collect_kernel(total, *refs):
    places, parts, out_ref, rows = refs[0], refs[1 : 1 + total], refs[-2], refs[-1]
    count = parts[0].shape[0]
    for j in range(total):
        rows[j * count : (j + 1) * count, :] = parts[j][...]
    out_ref[...] = dot_nn(places[...], rows[...]).astype(bf16)


def collect_rows(places, parts):
    tokens, count = places.shape
    rows, width = parts[0].shape
    block = 512 if width % 512 == 0 else 768
    return pl.pallas_call(
        functools.partial(collect_kernel, len(parts)),
        grid=(pl.cdiv(width, block),),
        in_specs=[pl.BlockSpec((tokens, count), lambda i: (0, 0))]
        + [pl.BlockSpec((rows, block), lambda i: (0, i))] * len(parts),
        out_specs=pl.BlockSpec((tokens, block), lambda i: (0, i)),
        out_shape=jax.ShapeDtypeStruct((tokens, width), bf16),
        scratch_shapes=[pltpu.VMEM((count, block), bf16)],
        compiler_params=pltpu.CompilerParams(vmem_limit_bytes=48 << 20),
        cost_estimate=pl.CostEstimate(
            flops=2 * tokens * count * width,
            bytes_accessed=2 * count * (width + tokens) + 2 * tokens * width,
            transcendentals=0,
        ),
    )(places, *parts)


def turn(values, cosine, sine):
    return values * cosine + pltpu.roll(values, HD // 2, 1) * sine


def head_forward(raw_q, raw_k, scale, gains, cosine, sine, row_pos, col_pos):
    query = turn(raw_q * scale[:, 0:1] * gains[0:1, :], cosine, sine).astype(bf16)
    key = turn(raw_k * scale[:, 1:2] * gains[1:2, :], cosine, sine).astype(bf16)
    scores = mm_nt(query, key) * (1.0 / math.sqrt(HD))
    scores = jnp.where(col_pos <= row_pos, scores, neg_large)
    weights = jnp.exp(scores - jnp.max(scores, -1, keepdims=True))
    return query, key, weights / jnp.sum(weights, -1, keepdims=True)


def project_kernel(place_ref, x_ref, w_ref, out_ref, square_ref):
    step = pl.program_id(0)
    part = dot_nn(x_ref[...], w_ref[...])

    @pl.when(step == 0)
    def _():
        out_ref[...] = part

    @pl.when(step > 0)
    def _():
        out_ref[...] += part

    @pl.when(step == pl.num_programs(0) - 1)
    def _():
        width = out_ref.shape[1] // 3
        for n in range(2):
            raw = out_ref[:, n * width : (n + 1) * width]
            square_ref[n : n + 1, :] = as_row(jnp.sum(raw * raw, -1, keepdims=True))


def project(place, x, w, total):
    seq, width = x.shape[0], x.shape[1] // total
    columns = w.shape[1] // total
    return pl.pallas_call(
        project_kernel,
        grid_spec=pltpu.PrefetchScalarGridSpec(
            num_scalar_prefetch=1,
            grid=(total,),
            in_specs=[
                pl.BlockSpec((seq, width), lambda j, s: (0, s[0] ^ j)),
                pl.BlockSpec((width, columns), lambda j, s: (0, j)),
            ],
            out_specs=[
                pl.BlockSpec((seq, columns), lambda j, s: (0, 0)),
                pl.BlockSpec((2, seq), lambda j, s: (0, 0)),
            ],
        ),
        out_shape=[
            jax.ShapeDtypeStruct((seq, columns), f32),
            jax.ShapeDtypeStruct((2, seq), f32),
        ],
        compiler_params=pltpu.CompilerParams(vmem_limit_bytes=48 << 20),
        cost_estimate=pl.CostEstimate(
            flops=2 * seq * x.shape[1] * columns,
            bytes_accessed=2 * x.size + 2 * w.size + 4 * seq * columns,
            transcendentals=0,
        ),
    )(place, x, w)


def project_back_kernel(place_ref, grad_ref, w_ref, out_ref):
    out_ref[...] = mm_nt(grad_ref[...], w_ref[...])


def project_back(place, grad, w, total):
    seq, columns = grad.shape
    width = w.shape[0]
    return pl.pallas_call(
        project_back_kernel,
        grid_spec=pltpu.PrefetchScalarGridSpec(
            num_scalar_prefetch=1,
            grid=(total,),
            in_specs=[
                pl.BlockSpec((seq, columns), lambda j, s: (0, 0)),
                pl.BlockSpec((width, columns), lambda j, s: (0, j)),
            ],
            out_specs=pl.BlockSpec((seq, width), lambda j, s: (0, s[0] ^ j)),
        ),
        out_shape=jax.ShapeDtypeStruct((seq, total * width), f32),
        compiler_params=pltpu.CompilerParams(vmem_limit_bytes=48 << 20),
        cost_estimate=pl.CostEstimate(
            flops=2 * seq * w.size,
            bytes_accessed=2 * grad.size + 2 * w.size + 4 * seq * total * width,
            transcendentals=0,
        ),
    )(place, grad, w)


def output_grad_kernel(x_ref, grad_ref, out_ref):
    out_ref[...] = mm_tn(x_ref[...], grad_ref[...]).astype(bf16)


def output_grad(x, grad, total):
    seq, width = x.shape
    return pl.pallas_call(
        output_grad_kernel,
        grid=(total,),
        in_specs=[
            pl.BlockSpec((seq, width), lambda j: (0, 0)),
            pl.BlockSpec((seq, width), lambda j: (0, j)),
        ],
        out_specs=pl.BlockSpec((width, width), lambda j: (0, 3 * total + j)),
        out_shape=jax.ShapeDtypeStruct((width, 4 * total * width), bf16),
        compiler_params=pltpu.CompilerParams(vmem_limit_bytes=48 << 20),
        cost_estimate=pl.CostEstimate(
            flops=2 * seq * total * width * width,
            bytes_accessed=4 * seq * total * width,
            transcendentals=0,
        ),
    )(x, grad)


def project_grad_kernel(place_ref, x_ref, grad_ref, held_ref, out_ref):
    out_ref[...] = mm_tn(x_ref[...], grad_ref[...]).astype(bf16)


def project_grad(place, x, grad, held, total):
    seq, columns = grad.shape
    width = x.shape[1] // total
    return pl.pallas_call(
        project_grad_kernel,
        grid_spec=pltpu.PrefetchScalarGridSpec(
            num_scalar_prefetch=1,
            grid=(total,),
            in_specs=[
                pl.BlockSpec((seq, width), lambda j, s: (0, s[0] ^ j)),
                pl.BlockSpec((seq, columns), lambda j, s: (0, 0)),
                pl.BlockSpec(memory_space=pl.ANY),
            ],
            out_specs=pl.BlockSpec((width, columns), lambda j, s: (0, j)),
        ),
        out_shape=jax.ShapeDtypeStruct(held.shape, bf16),
        input_output_aliases={3: 0},
        compiler_params=pltpu.CompilerParams(vmem_limit_bytes=48 << 20),
        cost_estimate=pl.CostEstimate(
            flops=2 * seq * x.shape[1] * columns,
            bytes_accessed=2 * x.size + 2 * grad.size + 2 * total * width * columns,
            transcendentals=0,
        ),
    )(place, x, grad, held)


def attend_kernel(model_width, q_ref, k_ref, v_ref, gain_ref, cos_ref, sin_ref, rp, cp, *refs):
    parts, out_ref, scale_ref = refs[:-2], refs[-2], refs[-1]

    @pl.when(pl.program_id(0) == 0)
    def _():
        scale = lax.rsqrt(add_rows(parts) / model_width + epsilon)
        for n in range(2):
            scale_ref[:, n : n + 1] = as_column(scale[n : n + 1, :])

    _, _, probs = head_forward(
        q_ref[...],
        k_ref[...],
        scale_ref[...],
        gain_ref[...],
        cos_ref[...],
        sin_ref[...],
        rp[...],
        cp[...],
    )
    out_ref[...] = dot_nn(probs.astype(bf16), v_ref[...].astype(bf16)).astype(bf16)


def attend_back_kernel(
    q_ref,
    k_ref,
    v_ref,
    gain_ref,
    cos_ref,
    sin_ref,
    rp,
    cp,
    scale_ref,
    grad_ref,
    yq_ref,
    yk_ref,
    gv_ref,
    dots_ref,
    gains_ref,
    held,
):
    head = pl.program_id(0)
    raw_q = q_ref[...]
    raw_k = k_ref[...]
    scale = scale_ref[...]
    gains = gain_ref[...]
    query, key, probs = head_forward(
        raw_q, raw_k, scale, gains, cos_ref[...], sin_ref[...], rp[...], cp[...]
    )
    grad = grad_ref[...]
    grad_prob = mm_nt(grad, v_ref[...].astype(bf16))
    delta = jnp.sum(probs * grad_prob, -1, keepdims=True)
    grad_scores = (probs * (grad_prob - delta)).astype(bf16)
    gv_ref[...] = mm_tn(probs.astype(bf16), grad).astype(bf16)
    soft = 1.0 / math.sqrt(HD)
    back_sine = -sin_ref[...]
    grad_q = turn(dot_nn(grad_scores, key) * soft, cos_ref[...], back_sine)
    grad_k = turn(mm_tn(grad_scores, query) * soft, cos_ref[...], back_sine)
    yq_ref[...] = grad_q
    yk_ref[...] = grad_k
    part_q = grad_q * raw_q
    part_k = grad_k * raw_k
    gains_ref[0:1, :] = jnp.sum(part_q * scale[:, 0:1], 0, keepdims=True)
    gains_ref[1:2, :] = jnp.sum(part_k * scale[:, 1:2], 0, keepdims=True)
    dot_q = jnp.sum(part_q * gains[0:1, :], -1, keepdims=True)
    dot_k = jnp.sum(part_k * gains[1:2, :], -1, keepdims=True)

    @pl.when(head == 0)
    def _():
        held[...] = jnp.zeros_like(held)

    held[:, 0:1] += dot_q
    held[:, 1:2] += dot_k

    @pl.when(head == pl.num_programs(0) - 1)
    def _():
        for n in range(2):
            dots_ref[n : n + 1, :] = as_row(held[:, n : n + 1])


def finish_kernel(model_width, heads, yq_ref, yk_ref, gv_ref, raw_ref, gain_ref, scale_ref, *refs):
    parts, out_ref, dots = refs[:-2], refs[-2], refs[-1]
    step = pl.program_id(0)

    @pl.when(step == 0)
    def _():
        total = add_rows(parts) / model_width
        for n in range(2):
            dots[:, n : n + 1] = as_column(total[n : n + 1, :])

    def through(n, grad):
        scale = scale_ref[:, n : n + 1]
        cube = scale * scale * scale * dots[:, n : n + 1]
        out_ref[...] = (scale * (grad * gain_ref[n : n + 1, :]) - raw_ref[...] * cube).astype(bf16)

    @pl.when(step < heads)
    def _():
        through(0, yq_ref[...])

    @pl.when((step >= heads) & (step < 2 * heads))
    def _():
        through(1, yk_ref[...])

    @pl.when(step >= 2 * heads)
    def _():
        out_ref[...] = gv_ref[...]


def finish(model_width, yq, yk, gv, raw_qkv, gains, scales, parts):
    seq, width = gv.shape
    heads = width // HD

    def block(first, last):
        return pl.BlockSpec((seq, HD), lambda i: (0, jnp.clip(i - first, 0, last)))

    return pl.pallas_call(
        functools.partial(finish_kernel, model_width, heads),
        grid=(3 * heads,),
        in_specs=[
            block(0, heads - 1),
            block(heads, heads - 1),
            block(2 * heads, heads - 1),
            block(0, 2 * heads - 1),
            pl.BlockSpec((2, HD), lambda i: (0, lax.rem(i, heads))),
            pl.BlockSpec((seq, 2), lambda i: (0, 0)),
        ]
        + [pl.BlockSpec((2, seq), lambda i: (0, 0))] * len(parts),
        out_specs=pl.BlockSpec((seq, HD), lambda i: (0, i)),
        out_shape=jax.ShapeDtypeStruct((seq, 3 * width), bf16),
        scratch_shapes=[pltpu.VMEM((seq, 2), f32)],
        compiler_params=pltpu.CompilerParams(vmem_limit_bytes=48 << 20),
        cost_estimate=pl.CostEstimate(
            flops=16 * seq * width, bytes_accessed=26 * seq * width, transcendentals=0
        ),
    )(yq, yk, gv, raw_qkv, gains, scales, *parts)


def head_specs(seq, heads):
    one = pl.BlockSpec((seq, HD), lambda h: (0, h))
    key = pl.BlockSpec((seq, HD), lambda h: (0, heads + h))
    value = pl.BlockSpec((seq, HD), lambda h: (0, 2 * heads + h))

    def fixed(shape):
        return pl.BlockSpec(shape, lambda h: (0, 0))

    specs = [
        one,
        key,
        value,
        pl.BlockSpec((2, HD), lambda h: (0, h)),
        fixed((seq, HD)),
        fixed((seq, HD)),
        fixed((seq, 1)),
        fixed((1, seq)),
    ]
    return one, specs, fixed


def attend(raw_qkv, tables, parts, model_width):
    seq = raw_qkv.shape[0]
    width = raw_qkv.shape[1] // 3
    heads = width // HD
    one, specs, fixed = head_specs(seq, heads)
    return pl.pallas_call(
        functools.partial(attend_kernel, model_width),
        grid=(heads,),
        in_specs=specs + [fixed((2, seq))] * len(parts),
        out_specs=[one, fixed((seq, 2))],
        out_shape=[
            jax.ShapeDtypeStruct((seq, width), bf16),
            jax.ShapeDtypeStruct((seq, 2), f32),
        ],
        compiler_params=pltpu.CompilerParams(vmem_limit_bytes=48 << 20),
        cost_estimate=pl.CostEstimate(
            flops=4 * seq * seq * width,
            bytes_accessed=12 * seq * width,
            transcendentals=seq * seq * heads,
        ),
    )(raw_qkv, raw_qkv, raw_qkv, *tables, *parts)


def attend_back(raw_qkv, tables, scales, grad):
    seq, width = grad.shape
    heads = width // HD
    one, specs, fixed = head_specs(seq, heads)
    return pl.pallas_call(
        attend_back_kernel,
        grid=(heads,),
        in_specs=specs + [fixed((seq, 2)), one],
        out_specs=[one, one, one, fixed((2, seq)), pl.BlockSpec((2, HD), lambda h: (0, h))],
        out_shape=[
            jax.ShapeDtypeStruct((seq, width), f32),
            jax.ShapeDtypeStruct((seq, width), f32),
            jax.ShapeDtypeStruct((seq, width), bf16),
            jax.ShapeDtypeStruct((2, seq), f32),
            jax.ShapeDtypeStruct((2, width), f32),
        ],
        scratch_shapes=[pltpu.VMEM((seq, 2), f32)],
        compiler_params=pltpu.CompilerParams(vmem_limit_bytes=56 << 20),
        cost_estimate=pl.CostEstimate(
            flops=12 * seq * seq * width,
            bytes_accessed=24 * seq * width,
            transcendentals=seq * seq * heads,
        ),
    )(raw_qkv, raw_qkv, raw_qkv, *tables, scales, grad)


def layer(
    tokens,
    attn_gain,
    query_gain,
    key_gain,
    w_query,
    w_key,
    w_value,
    output_weight,
    ffn_gain,
    router,
    experts,
    routes,
    cotangent,
):
    row_total = tokens.shape[1]
    half_rows = row_total // 2
    model_width = tokens.shape[2]
    expert_total = router.shape[1]
    slice_rows = experts.shape[0]
    local_experts = experts.shape[1]
    top_count = routes.shape[2]
    ff = experts.shape[2] // 3
    C = lax.axis_size(CTX)
    F = lax.axis_size(FSDP)
    devices = C * F
    W = model_width // C
    seq = C * row_total
    pieces = C // local_experts
    cap_unit = 16 * expert_total * pieces
    piece_cap = (17 * row_total * top_count + cap_unit - 1) // cap_unit
    me = lax.axis_index(CTX)
    row = lax.axis_index(FSDP)
    my_expert = row * local_experts + me // pieces
    my_column = me * W

    tokens_low = tokens.reshape(row_total, model_width)
    tokens_seq = gather_rows(tokens_low, C)
    route_ids = routes.reshape(row_total, top_count)
    column_ids = lax.all_gather(route_ids, FSDP, axis=0, tiled=True)

    blocks = []
    for j in range(C):
        piece = jnp.concatenate(
            [
                lax.dynamic_slice_in_dim(w, (me ^ j) * W, W, 1)
                for w in (w_query, w_key, w_value)
            ],
            1,
        )
        blocks.append(from_peer(piece, j, C) if j else piece)
    w_qkv = lax.all_gather(jnp.concatenate(blocks, 1), FSDP, axis=0, tiled=True)
    w_o = lax.all_gather(output_weight, FSDP, axis=0, tiled=True)

    by_expert = lax.optimization_barrier(
        jnp.swapaxes(lax.optimization_barrier(experts), 0, 1)
    )
    half = slice_rows // 2

    def expert_slice(array, j, begin, rows):
        first = ((me ^ j) // pieces, begin, 0)
        return lax.dynamic_slice(array, first, (1, rows, 3 * ff)).reshape(rows, 3 * ff)

    near = [j for j in range(1, C) if j & (j - 1) == 0]
    far = [j for j in range(1, C) if j not in near]
    eighth = slice_rows // 8
    near_cuts = [(j, part * half, half) for part in range(2) for j in near]
    far_cuts = [(j, part * eighth, eighth) for part in range(8) for j in far]
    cut = [expert_slice(by_expert, *o) for o in near_cuts]
    cut, later_expert = lax.optimization_barrier((cut, by_expert))
    own = [later_expert] * 2
    order = [(0, 0, half), (0, half, half)]
    for o, piece in zip(near_cuts, cut):
        order.append(o)
        own.append(from_peer(piece, o[0], C))
    for o in far_cuts:
        order.append(o)
        piece = expert_slice(later_expert, *o)
        own.append(from_peer(piece, o[0], C))
    expert = place_parts(me.reshape(1), pieces, tuple(order), own, slice_rows)

    column_rows = F * row_total
    member = jnp.sum(
        (column_ids[:, :, None] == jnp.arange(expert_total, dtype=jnp.int32)).astype(f32), 1
    )
    order = jnp.arange(row_total, dtype=jnp.int32)
    earlier = jnp.einsum(
        "ts,fse->fte",
        (order[None, :] < order[:, None]).astype(bf16),
        member.astype(bf16).reshape(F, row_total, expert_total),
        preferred_element_type=f32,
    ).reshape(column_rows, expert_total)
    marked = jnp.where(member > 0.5, earlier, -1.0).T
    group_rows = F * piece_cap
    group_ids = jnp.arange(group_rows, dtype=jnp.int32)
    token_block = jnp.arange(column_rows, dtype=jnp.int32) // row_total
    same_block = (group_ids // piece_cap)[:, None] == token_block[None, :]
    selects = []
    places = []
    for j in range(C):
        target = me ^ j
        mark = lax.dynamic_slice_in_dim(marked, row * local_experts + target // pieces, 1, 0)
        slot = (target % pieces) * piece_cap + group_ids % piece_cap
        slot = slot.astype(f32)
        selects.append(((mark == slot[:, None]) & same_block).astype(bf16))
        places.append(((mark.T == slot[None, :]) & same_block.T).astype(bf16))

    def exchange(parts):
        result = []
        for j in range(C):
            if j == 0:
                result.append(parts[j])
            else:
                result.append(from_peer(parts[j], j, C))
        return result

    def deliver(values):
        parts = [mm(select, values).astype(bf16) for select in selects]
        return exchange(parts)

    def collect(parts):
        return collect_rows(places, parts)

    cot_low = cotangent.reshape(row_total, model_width)
    cot_column = lax.all_gather(cot_low, FSDP, axis=0, tiled=True)
    cot_rows = deliver(cot_column)

    place = me ^ jnp.arange(C, dtype=jnp.int32)
    within = jnp.arange(half_rows, dtype=jnp.int32)
    positions = jnp.concatenate(
        [
            place[:, None] * half_rows + within,
            (2 * C - 1 - place)[:, None] * half_rows + within,
        ],
        1,
    ).reshape(seq)
    cosine, sine = rope_tables(positions, HD)
    inputs_seq = tokens_seq.astype(f32)
    scale_one = inv_rms(inputs_seq)
    normed = (inputs_seq * scale_one * attn_gain).astype(bf16)
    gains = lax.dynamic_slice_in_dim(jnp.stack([query_gain, key_gain]), my_column, W, 1)
    places = jnp.concatenate(places, 1)
    w_qkv, selects, places = lax.optimization_barrier((w_qkv, selects, places))
    place = me.reshape(1)
    raw_qkv, squares = project(place, normed, w_qkv, C)
    squares = spread_rows(squares, C)
    signed_sine = jnp.where(jnp.arange(HD) < HD // 2, -1.0, 1.0) * sine
    tables = (gains, cosine, signed_sine, positions.reshape(seq, 1), positions.reshape(1, seq))
    attended, scales = attend(raw_qkv, tables, squares, model_width)
    inputs = tokens_low.astype(f32)
    hidden_one = inputs + scatter_rows(mm(attended, w_o), C)

    scale_two = inv_rms(hidden_one)
    ffn_in = (hidden_one * scale_two * ffn_gain).astype(bf16)
    probs = jax.nn.softmax(mm(ffn_in, router), -1)
    ffn_column = lax.all_gather(ffn_in, FSDP, axis=0, tiled=True)
    expert_in = deliver(ffn_column)
    extra = -(-2 * expert_total // 128) * 128
    done = []
    mine = my_expert.reshape(1)
    for j in range(C):
        result = run_expert(mine, expert_in[j], cot_rows[j], router, expert, extra)
        if j == 0:
            result, mine = lax.optimization_barrier((result, mine))
        done.append(result)
    back = collect(exchange([d[0] for d in done]))
    back = lax.psum_scatter(back, FSDP, scatter_dimension=0, tiled=True).astype(f32)
    groups = [(expert_in[j], done[j][2], done[j][3], done[j][4], done[j][5]) for j in range(C)]
    d_own = []
    for j in range(C):
        d_own.append(weight_grad((me ^ j).reshape(1), groups, slice_rows))
    arrived = {}
    for j in range(C):
        for part in range(4):
            if j == 0:
                arrived[j, part] = d_own[j][part]
            else:
                arrived[j, part] = from_peer(d_own[j][part], j, C)
    d_experts = None
    for part in range(2):
        d_experts = merge_parts(
            (me // pieces).reshape(1),
            [arrived[j, 2 * part + n] for j in range(C) for n in range(2)],
            local_experts,
            part * half,
            slice_rows,
            d_experts,
        )
    mixed = collect(exchange([d[1] for d in done]))
    mixed = lax.psum_scatter(mixed, FSDP, scatter_dimension=0, tiled=True).astype(f32)

    grad_probs = (
        back[:, model_width : model_width + expert_total]
        + back[:, model_width + expert_total : model_width + 2 * expert_total]
    )
    grad_logits = (probs * (grad_probs - jnp.sum(probs * grad_probs, -1, keepdims=True))).astype(
        bf16
    )
    grad_ffn = back[:, :model_width] + mm_nt(grad_logits, router)
    grad_router = mm_tn(grad_logits, ffn_in)
    grad_hidden_one, grad_ffn_gain = norm_back(grad_ffn, hidden_one, scale_two, ffn_gain)
    grad_hidden_one = grad_hidden_one + cot_low.astype(f32)
    share = model_width // devices
    sums = jnp.concatenate(
        [grad_router.reshape(devices, -1), grad_ffn_gain.reshape(devices, share)], 1
    )
    sums = jnp.sum(lax.all_to_all(sums[:, None], everyone, 0, 0, tiled=True), 0)
    sums = lax.all_to_all(
        jnp.broadcast_to(sums, (devices,) + sums.shape), everyone, 0, 0, tiled=True
    ).reshape(devices, -1)
    d_ffn_gain = sums[:, -share:].reshape(model_width)
    d_router = sums[:, :-share].reshape(expert_total, model_width).T

    branch_seq = gather_rows(grad_hidden_one.astype(bf16), C)
    grad_att = mm_nt(branch_seq, w_o).astype(bf16)
    weight_sums = output_grad(attended, branch_seq, C)
    grad_q_n, grad_k_n, grad_value, dots, gain_grads = attend_back(
        raw_qkv, tables, scales, grad_att
    )
    dots = spread_rows(dots, C)
    late_hidden, dots = lax.optimization_barrier((hidden_one, dots))
    output = (late_hidden + mixed).astype(bf16).reshape(1, row_total, model_width)
    grad_qkv = finish(
        model_width, grad_q_n, grad_k_n, grad_value, raw_qkv, gains, scales, dots
    )
    weight_sums = lax.psum_scatter(
        project_grad(place, normed, grad_qkv, weight_sums, C),
        FSDP,
        scatter_dimension=0,
        tiled=True,
    )
    d_cols = weight_sums[:, : 3 * model_width]
    d_output = weight_sums[:, 3 * model_width :].astype(f32)
    received = []
    for j in range(C):
        piece = d_cols[:, 3 * W * j : 3 * W * (j + 1)]
        received.append(from_peer(piece, j, C) if j else piece)
    received = jnp.stack(received)
    received = [
        lax.dynamic_index_in_dim(received, me ^ c, 0, keepdims=False) for c in range(C)
    ]
    d_qkv = [
        jnp.concatenate([r[:, n * W : (n + 1) * W] for r in received], 1).astype(f32)
        for n in range(3)
    ]

    grad_normed = scatter_rows(project_back(place, grad_qkv, w_qkv, C), C)
    grad_inputs, grad_attn_gain = norm_back(grad_normed, inputs, scale_one[:row_total], attn_gain)
    grad_inputs = grad_inputs + grad_hidden_one

    vector = jnp.concatenate([grad_attn_gain, gain_grads[0], gain_grads[1]]).reshape(1, -1, 128)
    everything = lax.all_to_all(
        jnp.broadcast_to(vector, (devices,) + vector.shape[1:]), everyone, 0, 0, tiled=True
    ).reshape(devices, -1)
    d_attn_gain = jnp.sum(everything[:, :model_width], 0)
    by_place = jnp.sum(everything[:, model_width:].reshape(F, C, 2, W), 0)
    d_query_gain = by_place[:, 0].reshape(model_width)
    d_key_gain = by_place[:, 1].reshape(model_width)

    return (
        output,
        grad_inputs.reshape(1, row_total, model_width),
        d_attn_gain,
        d_query_gain,
        d_key_gain,
        d_qkv[0],
        d_qkv[1],
        d_qkv[2],
        d_output,
        d_ffn_gain,
        d_router,
        d_experts,
    )


def solution(mesh):
    placed = (
        P(FSDP, CTX, None),
        P(),
        P(),
        P(),
        P((CTX, FSDP), None),
        P((CTX, FSDP), None),
        P((CTX, FSDP), None),
        P((CTX, FSDP), None),
        P(),
        P(),
        P(CTX, FSDP, None),
        P(FSDP, CTX, None),
        P(FSDP, CTX, None),
    )
    return jax.shard_map(
        layer,
        mesh=mesh,
        in_specs=placed,
        out_specs=(
            P(FSDP, CTX, None),
            P(FSDP, CTX, None),
            P(),
            P(),
            P(),
            P((CTX, FSDP), None),
            P((CTX, FSDP), None),
            P((CTX, FSDP), None),
            P((CTX, FSDP), None),
            P(),
            P(),
            P(CTX, FSDP, None),
        ),
        check_vma=False,
    )
```
